256 devices in a mesh: gx: 16 (over x_lo, z), gz: 16 (over y, x_hi, core).
Axes of the slice: x: 4 (x_hi: 2, x_lo: 2; x = x_hi * 2 + x_lo), y: 4, z: 8, core: 2. Of those that a mesh axis runs over, the one named last changes fastest.
Arguments:
- conserved_fields: float32 [6, 256, 512, 128], P(None, 'gx', 'gz'), may hold values from -2 to 62, as said below
- coeff: bfloat16 [2, 1024, 6, 128, 512], P(None, 'gx', None, 'gz'), may hold values from -0.25 to 0.25
- feed_plane: int32 [25], replicated, may hold values from 0 to 2047
Outputs:
- new_state: float32 [6, 256, 512, 128], P(None, 'gx', 'gz')
The draws below stay inside these ranges and needn't reach their ends.
Inputs may be any that keep to these rules, and one draw needn't show every extreme that they name: `conserved_fields`: each cell is the conserved form of a gas with density 0.5 to 2, temperature 0.5 to 2, streamwise velocity -1 to 7, wall-normal and spanwise velocities -1 to 1 and vibrational energy per unit mass 0.05 to 0.5.
All inputs are finite; a program needn't handle non-finite values.
Results may differ from the reference program's by a relative error of at most 0.00038.
Values sent between devices are 32-bit elements; how exact they have to be, the bound alone decides.
A program may use at most 192 MiB of HBM per device.

```python
import math
import jax
import jax.numpy as jnp
from jax import lax

CX = 16
NY = 128
KXH = 1024
NZP = 512
NXP = 2048
NX = 256
NZ = 512
FORCE = 25
N_GX = 16


def draw_conserved_fields(key, part):
    stochastic_seeds = jax.random.split(jax.random.fold_in(key, 17), 6)
    field_extents = (NX, NZ, NY)
    fluid_rho_field = jax.random.uniform(stochastic_seeds[0], field_extents, jnp.float32, 0.5, 2.0)
    translational_kelvin = jax.random.uniform(stochastic_seeds[1], field_extents, jnp.float32, 0.5, 2.0)
    stream_vel = jax.random.uniform(stochastic_seeds[2], field_extents, jnp.float32, -1.0, 7.0)
    normal_vel = jax.random.uniform(stochastic_seeds[3], field_extents, jnp.float32, -1.0, 1.0)
    span_vel = jax.random.uniform(stochastic_seeds[4], field_extents, jnp.float32, -1.0, 1.0)
    oscillator_content = jax.random.uniform(stochastic_seeds[5], field_extents, jnp.float32, 0.05, 0.5)
    motion_share = 0.5 * (jnp.square(stream_vel) + jnp.square(normal_vel) + jnp.square(span_vel))
    overall_enthalpy_field = fluid_rho_field * (2.5 * translational_kelvin + motion_share + oscillator_content)
    return jnp.stack([fluid_rho_field, fluid_rho_field * stream_vel, fluid_rho_field * normal_vel, fluid_rho_field * span_vel, overall_enthalpy_field, fluid_rho_field * oscillator_content]).astype(jnp.float32)


def place_ends(entries, rng, low, top_value):
    longest = entries.shape.index(max(entries.shape))
    spots = []
    for shift in (0, 1):
        where = [jax.random.randint(jax.random.fold_in(rng, axis), (), 0, length) for axis, length in enumerate(entries.shape)]
        where[longest] = (where[longest] + shift) % entries.shape[longest]
        spots.append(tuple(where))
    return entries.at[spots[0]].set(low).at[spots[1]].set(top_value)


def level_of(rng, shape, cuts, least, high):
    level = 1.0
    for position, blocks in cuts:
        draws = jax.random.uniform(jax.random.fold_in(jax.random.fold_in(rng, 6), position), (blocks,), jnp.float32, least / len(cuts), high / len(cuts))
        level = level * jnp.repeat(jnp.exp(draws), shape[position] // blocks).reshape((-1,) + (1,) * (len(shape) - 1 - position))
    return level


def centred(stream_key, dims, deviation, most, shards=(), kind=jnp.bfloat16):
    level = level_of(stream_key, dims, shards, -0.22, 0.18) if shards else 1.0
    drawn = jax.random.normal(stream_key, dims, jnp.float32) * deviation * level
    return jnp.minimum(jnp.maximum(drawn, -most), most).astype(kind)


def setup_inputs(seed: int = 0) -> dict:
    key_list = jax.random.split(jax.random.key(seed), 4)
    return {
        "conserved_fields": draw_conserved_fields(jax.random.fold_in(key_list[3], 71), 0),
        "coeff": centred(key_list[1], (2, KXH, 6, NY, NZP), (KXH * NZP // 1024) ** -0.5, 0.25, ((1, 16), (3, 16))),
        "feed_plane": place_ends(jax.random.randint(key_list[2], (FORCE,), 0, NXP), jax.random.fold_in(key_list[2], 1), 0, NXP - 1).astype(jnp.int32),
    }


ADIABATIC_INDEX = 1.4
CAPACITY_CONST = 2.5
OSCILLATOR_SCALE = 2.0
VIBRANT_LAG = 0.5
LANDAU_FIT_LAW = 1.5
SURFACE_DIST_SQ = 0.36
TIME_STEP = 0.05
FORCING_RATE = 2.0
WENO_EPSILON = 1e-06

def caloric_bundle(conserved_fields):
    fluid_rho_field = conserved_fields[0]
    motion_share = 0.5 * (jnp.square(conserved_fields[1]) + jnp.square(conserved_fields[2]) + jnp.square(conserved_fields[3])) / jnp.square(fluid_rho_field)
    translational_kelvin = (conserved_fields[4] / fluid_rho_field - motion_share - conserved_fields[5] / fluid_rho_field) / CAPACITY_CONST
    thermodynamic_stress = fluid_rho_field * translational_kelvin
    return (fluid_rho_field, translational_kelvin, thermodynamic_stress)

def directional(extended_fields, component):
    fluid_rho_field, translational_kelvin, thermodynamic_stress = caloric_bundle(extended_fields)
    crossflow_flux_field = extended_fields[component] / fluid_rho_field
    flux_rows = []
    for member in range(6):
        entry = extended_fields[member] * crossflow_flux_field
        if member == component:
            entry = entry + thermodynamic_stress
        if member == 4:
            entry = entry + thermodynamic_stress * crossflow_flux_field
        flux_rows.append(entry)
    forcing_samples = jnp.abs(crossflow_flux_field) + jnp.sqrt(ADIABATIC_INDEX * translational_kelvin)
    return (jnp.stack(flux_rows), forcing_samples)

def weno_face(minus_two, minus_one, centre, plus_one, plus_two):
    low_poly = (2.0 * minus_two - 7.0 * minus_one + 11.0 * centre) / 6.0
    mid_poly = (-minus_one + 5.0 * centre + 2.0 * plus_one) / 6.0
    high_poly = (2.0 * centre + 5.0 * plus_one - plus_two) / 6.0
    low_beta = 13.0 / 12.0 * jnp.square(minus_two - 2.0 * minus_one + centre) + 0.25 * jnp.square(minus_two - 4.0 * minus_one + 3.0 * centre)
    mid_beta = 13.0 / 12.0 * jnp.square(minus_one - 2.0 * centre + plus_one) + 0.25 * jnp.square(minus_one - plus_one)
    high_beta = 13.0 / 12.0 * jnp.square(centre - 2.0 * plus_one + plus_two) + 0.25 * jnp.square(3.0 * centre - 4.0 * plus_one + plus_two)
    low_weight = 0.1 / jnp.square(WENO_EPSILON + low_beta)
    mid_weight = 0.6 / jnp.square(WENO_EPSILON + mid_beta)
    high_weight = 0.3 / jnp.square(WENO_EPSILON + high_beta)
    return (low_weight * low_poly + mid_weight * mid_poly + high_weight * high_poly) / (low_weight + mid_weight + high_weight)

def sweep_axis(extended_fields, axis, component):
    length = extended_fields.shape[axis] - 6
    fluxes, forcing_samples = directional(extended_fields, component)

    def window(array, offset, dim):
        return lax.slice_in_dim(array, offset, offset + length + 1, axis=dim)
    wave_speed = window(forcing_samples, 0, axis - 1)
    for offset in range(1, 6):
        wave_speed = jnp.maximum(wave_speed, window(forcing_samples, offset, axis - 1))
    wave_speed = wave_speed[None]
    upwind = [0.5 * (window(fluxes, offset, axis) + wave_speed * window(extended_fields, offset, axis)) for offset in range(5)]
    downwind = [0.5 * (window(fluxes, offset, axis) - wave_speed * window(extended_fields, offset, axis)) for offset in (5, 4, 3, 2, 1)]
    face_flux = weno_face(*upwind) + weno_face(*downwind)
    return lax.slice_in_dim(face_flux, 1, length + 1, axis=axis) - lax.slice_in_dim(face_flux, 0, length, axis=axis)

def wall_pad(conserved_fields):
    reflected_fields = conserved_fields[:, :, :, 2::-1]
    translational_kelvin = caloric_bundle(reflected_fields)[1]
    ghost_layer_kelvin = SURFACE_DIST_SQ / translational_kelvin
    ghost_layer_oscillator = reflected_fields[4] - CAPACITY_CONST * reflected_fields[0] * (translational_kelvin - ghost_layer_kelvin)
    ghost_cells = jnp.stack([reflected_fields[0], -reflected_fields[1], -reflected_fields[2], -reflected_fields[3], ghost_layer_oscillator, reflected_fields[5]])
    top_cells = jnp.repeat(conserved_fields[:, :, :, -1:], 3, axis=3)
    return jnp.concatenate([ghost_cells, conserved_fields, top_cells], axis=3)

def relaxation(conserved_fields):
    fluid_rho_field, translational_kelvin, thermodynamic_stress = caloric_bundle(conserved_fields)
    balanced_oscillator_share = OSCILLATOR_SCALE / (jnp.exp(OSCILLATOR_SCALE / translational_kelvin) - 1.0)
    settling_interval = VIBRANT_LAG * jnp.exp(LANDAU_FIT_LAW * (jnp.exp(-jnp.log(translational_kelvin) / 3.0) - 1.0)) / thermodynamic_stress
    return (fluid_rho_field * balanced_oscillator_share - conserved_fields[5]) / settling_interval

def precursor_feed(coeff, feed_plane):
    span_ids = jnp.arange(NZP, dtype=jnp.int32)[:, None] * jnp.arange(NZ, dtype=jnp.int32)[None, :] % NZP
    span_angle = 2.0 * math.pi / NZP * span_ids.astype(jnp.float32)
    span_table = jnp.concatenate([jnp.cos(span_angle), jnp.sin(span_angle)], axis=1).astype(jnp.bfloat16)
    span_table = lax.optimization_barrier(span_table).astype(jnp.float32)
    stream_ids = feed_plane[:, None] * jnp.arange(KXH, dtype=jnp.int32)[None, :] % NXP
    stream_angle = 2.0 * math.pi / NXP * stream_ids.astype(jnp.float32)
    stream_table = jnp.concatenate([jnp.cos(stream_angle), -jnp.sin(stream_angle)], axis=1).astype(jnp.bfloat16)
    stream_table = lax.optimization_barrier(stream_table).astype(jnp.float32)

    def one_variable(block):
        coeff_rows = block.reshape(2 * KXH * NY, NZP).astype(jnp.float32)
        product = jnp.dot(coeff_rows, span_table, precision=lax.Precision.HIGHEST).reshape(2, KXH, NY, 2 * NZ)
        real_part = product[0, :, :, :NZ] - product[1, :, :, NZ:]
        imag_part = product[0, :, :, NZ:] + product[1, :, :, :NZ]
        mixed_modes = jnp.concatenate([real_part, imag_part], axis=0).astype(jnp.bfloat16)
        mixed_modes = lax.optimization_barrier(mixed_modes).astype(jnp.float32)
        summed = jnp.dot(stream_table, mixed_modes.reshape(2 * KXH, NY * NZ), precision=lax.Precision.HIGHEST)
        return summed.reshape(FORCE, NY, NZ)
    feed_values = lax.map(one_variable, jnp.moveaxis(coeff, 2, 0))
    return jnp.transpose(feed_values, (0, 1, 3, 2))

def reference(conserved_fields, coeff, feed_plane):
    stream_pad = jnp.concatenate([jnp.repeat(conserved_fields[:, :1], 3, axis=1), conserved_fields, jnp.repeat(conserved_fields[:, -1:], 3, axis=1)], axis=1)

    def block_rate(start):
        block = lax.dynamic_slice_in_dim(stream_pad, start, CX + 6, axis=1)
        interior = block[:, 3:-3]
        span_pad = jnp.concatenate([interior[:, :, -3:], interior, interior[:, :, :3]], axis=2)
        tendency = -(sweep_axis(block, 1, 1) + sweep_axis(span_pad, 2, 3) + sweep_axis(wall_pad(interior), 3, 2))
        return tendency.at[5].add(relaxation(interior))
    starts = jnp.arange(N_GX, dtype=jnp.int32) * CX
    blocks = lax.map(block_rate, starts)
    tendency = jnp.moveaxis(blocks, 0, 1).reshape(6, NX, NZ, NY)
    target = precursor_feed(coeff, feed_plane)
    plane_pos = jnp.arange(FORCE, dtype=jnp.int32).astype(jnp.float32)
    strength = FORCING_RATE * jnp.square(1.0 - plane_pos / FORCE)
    forcing = strength[None, :, None, None] * (target - conserved_fields[:, :FORCE])
    tendency = tendency.at[:, :FORCE].add(forcing)
    return conserved_fields + TIME_STEP * tendency
```

```python
import math

import jax, jax.numpy as jnp
from jax import lax
from jax.experimental import pallas as pl
from jax.experimental.pallas import tpu as pltpu
from jax.sharding import PartitionSpec as P
import numpy as np

F32 = jnp.float32
NXL, NZL, NYL = 16, 32, 128


def flux_parts(q, n):
    r, m1, m2, m3, en, ev = q
    rinv = 1.0 / r
    un = q[n] * rinv
    ke = (m1 * m1 + m2 * m2 + m3 * m3) * (0.5 * rinv)
    p = (en - ke - ev) * (1.0 / 2.5)
    s = jnp.abs(un) + jnp.sqrt(1.4 * (p * rinv))
    h = 0.5 * un
    g = [q[c] * h for c in range(6)]
    g[n] = g[n] + 0.5 * p
    g[4] = g[4] + p * h
    return g, 0.5 * s


def ratio(num, den):
    return num * pl.reciprocal(den, approx=False)


def correction(d2, d3, e0, e1, e2):
    d2s = d2 * d2 + 1e-6
    b0 = d2s + e0 * (d2 + (4.0 / 3.0) * e0)
    b1 = d2s + e1 * (d2 + (4.0 / 3.0) * e1)
    b2 = (d3 * d3 + 1e-6) + e2 * ((4.0 / 3.0) * e2 - d3)
    p0, p1, p2 = b0 * b0, b1 * b1, b2 * b2
    w0 = p1 * p2
    w1 = 6.0 * (p0 * p2)
    w2 = 3.0 * (p0 * p1)
    num = e0 * w0 + e1 * w1 + (e1 + 0.5 * (e1 - e2)) * w2
    return ratio(num, w0 + w1 + w2)


def face_value(a, gs, dg, dq, eg, eq):
    ad = [a * x for x in dq]
    ae = [a * x for x in eq]
    pd2, pd3 = dg[0] + ad[0], dg[1] + ad[1]
    md2, md3 = ad[2] - dg[2], ad[1] - dg[1]
    pe = [eg[i] + ae[i] for i in (0, 1, 2)]
    me = [eg[i] - ae[i] for i in (3, 2, 1)]
    lead = (gs - ad[1]) + 0.5 * (pd2 + md2)
    return lead + (1.0 / 3.0) * (correction(pd2, pd3, *pe) + correction(md2, md3, *me))


def face_sweep(qr, gr, ar, tr, comps, n, rows, unroll, tick):
    chunks = rows // 8

    def outer(t, _):
        c = t // chunks
        r0 = (t % chunks) * 8
        at = lambda ref, i: ref[c, pl.ds(pl.multiple_of(i * rows + r0, 8), 8), :]

        def advance(state, f):
            dq, dg, eq, eg = state
            dqn = at(qr, f + 5) - at(qr, f + 4)
            dgn = at(gr, f + 5) - at(gr, f + 4)
            eqn, egn = dqn - dq[2], dgn - dg[2]
            return (dq[0], dq[1], dq[2], dqn), (dg[0], dg[1], dg[2], dgn), (*eq, eqn), (*eg, egn)

        def one(state, f):
            dq, dg, eq, eg = advance(state, f)
            a = ar[pl.ds(pl.multiple_of(f * rows + r0, 8), 8), :]
            gs = at(gr, f + 2) + at(gr, f + 3)
            val = face_value(a, gs, dg[:3], dq[:3], eg, eq)
            return (dq[1:], dg[1:], eq[1:], eg[1:]), val

        qs = [at(qr, i) for i in range(5)]
        gs = [at(gr, i) for i in range(5)]
        dq = [qs[i + 1] - qs[i] for i in range(4)]
        dg = [gs[i + 1] - gs[i] for i in range(4)]
        eq = [dq[i + 1] - dq[i] for i in range(3)]
        eg = [dg[i + 1] - dg[i] for i in range(3)]
        state = (tuple(dq[1:]), tuple(dg[1:]), tuple(eq), tuple(eg))
        state, prev = one(state, 0)

        def inner(b, carry):
            state, prev = carry
            for k in range(unroll):
                f = b * unroll + k + 1
                state, val = one(state, f)
                tr[c, pl.ds(pl.multiple_of((f - 1) * rows + r0, 8), 8), :] = val - prev
                prev = val
            tick(t * (n // unroll) + b)
            return state, prev

        lax.fori_loop(0, n // unroll, inner, (state, prev))
        return 0

    lax.fori_loop(0, comps * chunks, outer, 0)


def speed_sweep(sr, ar, n, rows):
    def body(f, _):
        for r0 in range(0, rows, 8):
            ld = lambda i: sr[pl.ds(pl.multiple_of(i * rows + r0, 8), 8), :]
            m = ld(f)
            for o in range(1, 6):
                m = jnp.maximum(m, ld(f + o))
            ar[pl.ds(pl.multiple_of(f * rows + r0, 8), 8), :] = m
        return 0

    lax.fori_loop(0, n + 1, body, 0)


def flux_sweep(qr, gr, sr, first, count, normal):
    def body(i, _):
        at = pl.ds(pl.multiple_of(i * 8, 8), 8)
        g, s = flux_parts([qr[c, at, :] for c in range(6)], normal)
        for c in range(6):
            gr[c, at, :] = g[c]
        sr[at, :] = s
        return 0

    lax.fori_loop(first, first + count, body, 0, unroll=2)


def transpose_in(qx, tq, qy, gy, sy, tick):
    def block(blk, _):
        for c in range(6):
            x = qx[c, pl.ds(pl.multiple_of(96 + blk * 128, 32), 128), :]
            tq[c] = x.T

        def rows(y, _):
            y0 = pl.multiple_of(y * 8, 8)
            q = [tq[c, pl.ds(y0, 8), :] for c in range(6)]
            g, s = flux_parts(q, 2)
            base = (3 + y0) * 8
            for c in range(6):
                spot = pl.ds(base + (c % 2) * 4 + blk, 8, stride=8)
                qy[c // 2, spot, :] = q[c]
                gy[c // 2, spot, :] = g[c]
            sy[pl.ds(base + blk, 8, stride=8), :] = s
            sy[pl.ds(base + 4 + blk, 8, stride=8), :] = s
            return 0

        lax.fori_loop(0, 16, rows, 0)
        r, m1, m2, m3, en, ev = [tq[c, 0:8, :] for c in range(6)]
        rinv = 1.0 / r
        ke = (m1 * m1 + m2 * m2 + m3 * m3) * (0.5 * rinv)
        temp = (en - ke - ev) * (1.0 / 2.5) * rinv
        ghost = [r, -m1, -m2, -m3, en - 2.5 * r * (temp - 0.36 / temp), ev]
        g, s = flux_parts(ghost, 2)
        for k in range(3):
            for c in range(6):
                spot = pl.ds((2 - k) * 8 + (c % 2) * 4 + blk, 1)
                qy[c // 2, spot, :] = ghost[c][k : k + 1]
                gy[c // 2, spot, :] = g[c][k : k + 1]
            sy[pl.ds((2 - k) * 8 + blk, 1), :] = s[k : k + 1]
            sy[pl.ds((2 - k) * 8 + 4 + blk, 1), :] = s[k : k + 1]
        tick(blk)
        return 0

    lax.fori_loop(0, 4, block, 0)
    for k in range(3):
        src, dst = pl.ds(130 * 8, 8), pl.ds((131 + k) * 8, 8)
        for c in range(3):
            qy[c, dst, :] = qy[c, src, :]
            gy[c, dst, :] = gy[c, src, :]
        sy[dst, :] = sy[src, :]


def swap_in(qx, qz):
    def body(z, _):
        for c in range(6):
            for x0 in (0, 8):
                v = qx[c, pl.ds((3 + x0) * 32 + z, 8, stride=32), :]
                qz[c, pl.ds(pl.multiple_of((3 + z) * 16 + x0, 8), 8), :] = v
        return 0

    lax.fori_loop(0, 32, body, 0)


def combine(qx, tx, tz, ty, out, strength):
    def block(blk, _):
        for c in range(6):
            t = ty[c // 2, pl.ds((c % 2) * 4 + blk, 128, stride=8), :].T
            for k in range(4):
                x = blk * 4 + k
                span = tz[c, pl.ds(x, 32, stride=16), :]
                at = pl.ds(pl.multiple_of(x * 32, 32), 32)
                q = qx[c, pl.ds(pl.multiple_of(96 + x * 32, 32), 32), :]
                rate = tx[c, at, :] + span + t[k * 32 : k * 32 + 32] + strength(x) * q
                out[c, at, :] = q - 0.05 * rate
        return 0

    lax.fori_loop(0, 4, block, 0)

    def relax(i, _):
        at = pl.ds(pl.multiple_of(96 + i * 8, 8), 8)
        r, m1, m2, m3, en, ev = [qx[c, at, :] for c in range(6)]
        rinv = 1.0 / r
        ke = (m1 * m1 + m2 * m2 + m3 * m3) * (0.5 * rinv)
        p = (en - ke - ev) * (1.0 / 2.5)
        temp = p * rinv
        eq = 2.0 / (jnp.exp(2.0 / temp) - 1.0)
        tau = 0.5 * jnp.exp(1.5 * (jnp.exp(jnp.log(temp) * (-1.0 / 3.0)) - 1.0))
        dst = pl.ds(pl.multiple_of(i * 8, 8), 8)
        out[5, dst, :] = out[5, dst, :] + 0.05 * ((r * eq - ev) * p / tau)
        return 0

    lax.fori_loop(0, 64, relax, 0, unroll=2)


def weno_scratch():
    v = lambda *s: pltpu.VMEM(s, F32)
    return dict(
        qx=v(6, 22 * 32, 128), gx=v(6, 22 * 32, 128), sx=v(22 * 32, 128), ax=v(17 * 32, 128), tx=v(6, 16 * 32, 128),
        qz=v(6, 38 * 16, 128), gz=v(6, 38 * 16, 128), sz=v(38 * 16, 128), az=v(33 * 16, 128), tz=v(6, 32 * 16, 128),
        tq=v(6, 128, 128), qy=v(3, 134 * 8, 128), gy=v(3, 134 * 8, 128), sy=v(134 * 8, 128), ay=v(129 * 8, 128), ty=v(3, 128 * 8, 128),
    )


MESH = pl.DeviceIdType.MESH
PLANES = 25
STEP, HOP = 2, 4
PIECES = 48
WIRE_TICKS = PIECES * STEP + 7 * HOP


def spectral_kernel(coeff, table, kron, out, acc):
    step = pl.program_id(0)
    both = jnp.concatenate([coeff[0], coeff[1]], axis=1)
    for half in range(2):
        lanes = slice(half * 256, half * 256 + 256)
        re = jnp.dot(both, table[:, half * 256 : half * 256 + 256], preferred_element_type=F32)
        im = jnp.dot(both, table[:, 512 + half * 256 : 768 + half * 256], preferred_element_type=F32)
        re = re.reshape(16, 6, 8, 256)
        im = im.reshape(16, 6, 8, 256)
        for v in range(6):
            modes = jnp.concatenate([re[:, v].reshape(128, 256), im[:, v].reshape(128, 256)], axis=0)
            part = jnp.dot(kron[0], modes.astype(jnp.bfloat16), preferred_element_type=F32)

            @pl.when(step == 0)
            def _():
                acc[v, :, lanes] = part

            @pl.when(step > 0)
            def _():
                acc[v, :, lanes] = acc[v, :, lanes] + part

    @pl.when(step == pl.num_programs(0) - 1)
    def _():
        lane = lax.broadcasted_iota(jnp.int32, (8, 128), 1)
        low64 = lane < 64
        low32 = lane % 64 < 32

        def tiles(t, _):
            v, g = t // 7, t % 7
            for jb in range(4):
                f = [acc[v, pl.ds(pl.multiple_of(g * 32 + i * 8, 8), 8), jb * 128 : jb * 128 + 128] for i in range(4)]
                n0 = jnp.where(low64, f[0], pltpu.roll(f[2], 64, 1))
                n2 = jnp.where(low64, pltpu.roll(f[0], 64, 1), f[2])
                n1 = jnp.where(low64, f[1], pltpu.roll(f[3], 64, 1))
                n3 = jnp.where(low64, pltpu.roll(f[1], 64, 1), f[3])
                for k, (a, b) in enumerate(((n0, n1), (n2, n3))):
                    out[4 * jb + 2 * k, v, g] = jnp.where(low32, a, pltpu.roll(b, 32, 1))
                    out[4 * jb + 2 * k + 1, v, g] = jnp.where(low32, pltpu.roll(a, 96, 1), b)
            return 0

        lax.fori_loop(0, 42, tiles, 0)


def spectral(coeff, feed_plane):
    n = np.arange(512)
    angle = 2.0 * np.pi / 512.0 * ((n[:, None] * n[None, :]) % 512)
    cz, sz = np.cos(angle), np.sin(angle)
    table = jnp.asarray(np.block([[cz, sz], [-sz, cz]]).astype(np.float32)).astype(jnp.bfloat16)
    shape = (4, 224, 256)
    step, row, col = (lax.broadcasted_iota(jnp.int32, shape, d) for d in range(3))
    feed = jnp.pad(feed_plane, (0, 28 - PLANES))
    feed = jnp.broadcast_to(feed[:, None], (28, 8)).reshape(1, 224, 1)
    mode = lax.axis_index("gx") * 64 + step * 16 + (col % 128) // 8
    ids = (feed * mode + 512 * (col // 128)) % 2048
    wave = jnp.cos(2.0 * math.pi / 2048 * ids.astype(F32))
    kron = jnp.where((row % 8 == col % 8) & (row < 8 * PLANES), wave, 0.0).astype(jnp.bfloat16)
    return pl.pallas_call(
        spectral_kernel,
        grid=(4,),
        out_shape=jax.ShapeDtypeStruct((16, 6, 7, 8, 128), F32),
        in_specs=[
            pl.BlockSpec((2, 768, 512), lambda i: (0, i, 0)),
            pl.BlockSpec((1024, 1024), lambda i: (0, 0)),
            pl.BlockSpec((1, 224, 256), lambda i: (i, 0, 0)),
        ],
        out_specs=pl.BlockSpec((16, 6, 7, 8, 128), lambda i: (0, 0, 0, 0, 0)),
        scratch_shapes=[pltpu.VMEM((6, 224, 512), F32)],
        compiler_params=pltpu.CompilerParams(dimension_semantics=("arbitrary",), vmem_limit_bytes=56 * 2**20),
    )(coeff.reshape(2, 3072, 512), table, kron)


def main_kernel(names, q_hbm, part, out, *scratch):
    s = dict(zip(names, scratch))
    qx, qz, land, feed = s["qx"], s["qz"], s["land"], s["feed"]
    gx, gz = lax.axis_index("gx"), lax.axis_index("gz")
    z, xlo = gx % 8, gx // 8
    z_next = {0: xlo * 8 + (z + 1) % 8, 1: xlo * 8 + (z + 7) % 8}
    is_root = z < 2

    load = pltpu.make_async_copy(q_hbm, qx.at[:, 96:608], s["load_sem"])
    load.start()

    barrier = pltpu.get_barrier_semaphore()

    def greet(a, b):
        pl.semaphore_signal(barrier, inc=1, device_id=(a, b), device_id_type=MESH)

    @pl.when(gx < 15)
    def _():
        greet(gx + 1, gz)

    @pl.when(gx > 0)
    def _():
        greet(gx - 1, gz)

    greet(z_next[0], gz)
    greet(z_next[1], gz)
    greet(gx, (gz + 1) % 16)
    greet(gx, (gz + 15) % 16)

    @pl.when(is_root)
    def _():
        def each(b, _):
            @pl.when((xlo == 1) | (b != gz))
            def _():
                greet(z, b)

            @pl.when(xlo == 0)
            def _():
                greet(8 + z, b)

            return 0

        lax.fori_loop(0, 16, each, 0)

    ends = jnp.where((gx == 0) | (gx == 15), 1, 0)
    roots = jnp.where(is_root, jnp.where(xlo == 0, 31, 16), 0)
    pl.semaphore_wait(barrier, 6 - ends + roots)

    def remote(src, dst, ssem, rsem, a, b):
        return pltpu.make_async_remote_copy(
            src_ref=src, dst_ref=dst, send_sem=ssem, recv_sem=rsem, device_id=(a, b), device_id_type=MESH
        )

    lines = []
    for r in range(2):
        for d in range(2):
            pos = (z - r + 15) % 8 if d == 0 else (r + 7 - z) % 8
            lines.append((r, d, pos))

    def piece(r, d, k):
        c = (gz + 8 * d + k // 6) % 16
        return c, k % 6, (slice(0, 4) if r == 0 else slice(4, 7))

    def tick(n):
        for line, (r, d, pos) in enumerate(lines):
            m = n - pos * HOP
            k = m // STEP

            @pl.when((m >= 0) & (m < PIECES * STEP) & (m % STEP == 0))
            def _():
                c, v, g = piece(r, d, k)
                mine, held = part.at[c, v, g], land.at[c, v, g]
                ssem, rsem = s["send_sem"].at[line], s["recv_sem"].at[line, k]
                onward = lambda src: remote(src, held, ssem, rsem, z_next[d], gz)

                @pl.when(pos == 0)
                def _():
                    onward(mine).start()

                @pl.when(pos > 0)
                def _():
                    onward(held).wait_recv()
                    held[...] = held[...] + mine[...]

                @pl.when((pos > 0) & (pos < 7))
                def _():
                    onward(held).start()

                @pl.when(pos == 7)
                def _():
                    place = feed.at[xlo, v, 0 : (4 if r == 0 else 3), gz]
                    here = (xlo == 0) & (c == gz)

                    @pl.when(here)
                    def _():
                        pltpu.make_async_copy(held, place, s["feed_sem"]).start()

                    @pl.when(jnp.logical_not(here))
                    def _():
                        remote(held, place, ssem, s["feed_sem"], r, c).start()

    halo = []
    for i, (src, dst, a, b, ok_send, ok_recv) in enumerate(
        (
            (qx.at[:, 512:608], qx.at[:, 0:96], jnp.minimum(gx + 1, 15), gz, gx < 15, gx > 0),
            (qx.at[:, 96:192], qx.at[:, 608:704], jnp.maximum(gx - 1, 0), gz, gx > 0, gx < 15),
            (qz.at[:, 512:560], qz.at[:, 0:48], gx, (gz + 1) % 16, None, None),
            (qz.at[:, 48:96], qz.at[:, 560:608], gx, (gz + 15) % 16, None, None),
        )
    ):
        halo.append((remote(src, dst, s["halo_send"].at[i], s["halo_recv"].at[i], a, b), ok_send, ok_recv))

    def on(ok, act):
        if ok is None:
            act()
        else:
            pl.when(ok)(act)

    load.wait()
    for copy, ok, _ in halo[:2]:
        on(ok, copy.start)
    swap_in(qx, qz)
    for copy, ok, _ in halo[2:]:
        on(ok, copy.start)
    transpose_in(qx, s["tq"], s["qy"], s["gy"], s["sy"], lambda blk: tick(blk))
    speed_sweep(s["sy"], s["ay"], 128, 8)
    face_sweep(s["qy"], s["gy"], s["ay"], s["ty"], 3, 128, 8, 8, lambda i: tick(i + 4))
    for copy, _, ok in halo[2:]:
        on(ok, copy.wait_recv)
    flux_sweep(qz, s["gz"], s["sz"], 0, 76, 3)
    speed_sweep(s["sz"], s["az"], 32, 16)
    face_sweep(qz, s["gz"], s["az"], s["tz"], 6, 32, 16, 8, lambda i: tick(i + 52))
    for copy, _, ok in halo[:2]:
        on(ok, copy.wait_recv)

    @pl.when(gx == 0)
    def _():
        for i in range(3):
            qx[:, i * 32 : i * 32 + 32] = qx[:, 96:128]

    @pl.when(gx == 15)
    def _():
        for i in range(3):
            qx[:, 608 + i * 32 : 640 + i * 32] = qx[:, 576:608]

    flux_sweep(qx, s["gx"], s["sx"], 0, 88, 1)
    speed_sweep(s["sx"], s["ax"], 16, 32)
    face_sweep(qx, s["gx"], s["ax"], s["tx"], 6, 16, 32, 16, lambda i: tick(i + 100))

    def strength(x):
        plane = gx * 16 + x
        level = 1.0 - plane.astype(F32) * (1.0 / PLANES)
        return jnp.where(plane < PLANES, 2.0 * level * level, 0.0)

    combine(qx, s["tx"], s["tz"], s["ty"], out, strength)

    def drain(n, _):
        tick(n)
        return 0

    lax.fori_loop(124, WIRE_TICKS, drain, 0)

    for r in range(2):

        @pl.when(gx == r)
        def _():
            groups = 4 if r == 0 else 3
            whole = feed.at[:, :, 0:groups]
            pltpu.make_async_copy(whole, whole, s["feed_sem"]).wait()

            def add(v, _):
                for g in range(groups):
                    t = (feed[0, v, g].reshape(128, 128) + feed[1, v, g].reshape(128, 128)).T
                    for i in range(4):
                        x = g * 4 + i
                        at = slice(x * 32, x * 32 + 32)
                        out[v, at, :] = out[v, at, :] + (0.05 * strength(jnp.int32(x))) * t[i * 32 : i * 32 + 32]
                return 0

            lax.fori_loop(0, 6, add, 0)

    for copy, ok, _ in halo:
        on(ok, copy.wait_send)
    for line, (r, d, pos) in enumerate(lines):
        groups = slice(0, 4) if r == 0 else slice(4, 7)
        short = (pos == 7) & (xlo == 0) if d == 0 else None

        def sent(blocks):
            span = land.at[0:blocks, :, groups]
            pltpu.make_async_copy(span, span, s["send_sem"].at[line]).wait()

        if short is None:
            sent(8)
        else:
            pl.when(short)(lambda: sent(7))
            pl.when(jnp.logical_not(short))(lambda: sent(8))


def local(conserved_fields, coeff, feed_plane):
    part = spectral(coeff, feed_plane)
    scratch = weno_scratch()
    scratch.update(
        land=pltpu.VMEM((16, 6, 7, 8, 128), F32),
        feed=pltpu.VMEM((2, 6, 4, 16, 8, 128), F32),
        load_sem=pltpu.SemaphoreType.DMA,
        halo_send=pltpu.SemaphoreType.DMA((4,)),
        halo_recv=pltpu.SemaphoreType.DMA((4,)),
        send_sem=pltpu.SemaphoreType.DMA((4,)),
        recv_sem=pltpu.SemaphoreType.DMA((4, PIECES)),
        feed_sem=pltpu.SemaphoreType.DMA,
    )
    names = list(scratch)
    out = pl.pallas_call(
        lambda *refs: main_kernel(names, *refs),
        out_shape=jax.ShapeDtypeStruct((6, 512, 128), F32),
        in_specs=[pl.BlockSpec(memory_space=pl.ANY), pl.BlockSpec(memory_space=pltpu.VMEM)],
        out_specs=pl.BlockSpec(memory_space=pltpu.VMEM),
        scratch_shapes=list(scratch.values()),
        compiler_params=pltpu.CompilerParams(collective_id=0, has_side_effects=True, vmem_limit_bytes=56 * 2**20),
        name="section",
    )(conserved_fields.reshape(6, 512, 128), part)
    return out.reshape(6, 16, 32, 128)


def solution(mesh):
    placed = (P(None, "gx", "gz", None), P(None, "gx", None, "gz", None), P())
    return jax.shard_map(
        local, mesh=mesh, in_specs=placed, out_specs=P(None, "gx", "gz", None), check_vma=False
    )
```

```python
import math

import jax, jax.numpy as jnp
from jax import lax
from jax.experimental import pallas as pl
from jax.experimental.pallas import tpu as pltpu
from jax.sharding import PartitionSpec as P
import numpy as np

F32 = jnp.float32
NXL, NZL, NYL = 16, 32, 128


def flux_parts(q, n):
    r, m1, m2, m3, en, ev = q
    rinv = 1.0 / r
    un = q[n] * rinv
    ke = (m1 * m1 + m2 * m2 + m3 * m3) * (0.5 * rinv)
    p = (en - ke - ev) * (1.0 / 2.5)
    s = jnp.abs(un) + jnp.sqrt(1.4 * (p * rinv))
    h = 0.5 * un
    g = [q[c] * h for c in range(6)]
    g[n] = g[n] + 0.5 * p
    g[4] = g[4] + p * h
    return g, 0.5 * s


def ratio(num, den):
    return num * pl.reciprocal(den, approx=False)


def correction(d2, d3, e0, e1, e2):
    d2s = d2 * d2 + 1e-6
    b0 = d2s + e0 * (d2 + (4.0 / 3.0) * e0)
    b1 = d2s + e1 * (d2 + (4.0 / 3.0) * e1)
    b2 = (d3 * d3 + 1e-6) + e2 * ((4.0 / 3.0) * e2 - d3)
    p0, p1, p2 = b0 * b0, b1 * b1, b2 * b2
    w0 = p1 * p2
    w1 = 6.0 * (p0 * p2)
    w2 = 3.0 * (p0 * p1)
    num = e0 * w0 + e1 * w1 + (e1 + 0.5 * (e1 - e2)) * w2
    return ratio(num, w0 + w1 + w2)


def face_value(a, gs, dg, dq, eg, eq):
    ad = [a * x for x in dq]
    ae = [a * x for x in eq]
    pd2, pd3 = dg[0] + ad[0], dg[1] + ad[1]
    md2, md3 = ad[2] - dg[2], ad[1] - dg[1]
    pe = [eg[i] + ae[i] for i in (0, 1, 2)]
    me = [eg[i] - ae[i] for i in (3, 2, 1)]
    lead = (gs - ad[1]) + 0.5 * (pd2 + md2)
    return lead + (1.0 / 3.0) * (correction(pd2, pd3, *pe) + correction(md2, md3, *me))


def face_sweep(qr, gr, ar, tr, comps, n, rows, unroll, tick):
    chunks = rows // 8

    def outer(t, _):
        c = t // chunks
        r0 = (t % chunks) * 8
        at = lambda ref, i: ref[c, pl.ds(pl.multiple_of(i * rows + r0, 8), 8), :]

        def advance(state, f):
            dq, dg, eq, eg = state
            dqn = at(qr, f + 5) - at(qr, f + 4)
            dgn = at(gr, f + 5) - at(gr, f + 4)
            eqn, egn = dqn - dq[2], dgn - dg[2]
            return (dq[0], dq[1], dq[2], dqn), (dg[0], dg[1], dg[2], dgn), (*eq, eqn), (*eg, egn)

        def one(state, f):
            dq, dg, eq, eg = advance(state, f)
            a = ar[pl.ds(pl.multiple_of(f * rows + r0, 8), 8), :]
            gs = at(gr, f + 2) + at(gr, f + 3)
            val = face_value(a, gs, dg[:3], dq[:3], eg, eq)
            return (dq[1:], dg[1:], eq[1:], eg[1:]), val

        qs = [at(qr, i) for i in range(5)]
        gs = [at(gr, i) for i in range(5)]
        dq = [qs[i + 1] - qs[i] for i in range(4)]
        dg = [gs[i + 1] - gs[i] for i in range(4)]
        eq = [dq[i + 1] - dq[i] for i in range(3)]
        eg = [dg[i + 1] - dg[i] for i in range(3)]
        state = (tuple(dq[1:]), tuple(dg[1:]), tuple(eq), tuple(eg))
        state, prev = one(state, 0)

        def inner(b, carry):
            state, prev = carry
            for k in range(unroll):
                f = b * unroll + k + 1
                state, val = one(state, f)
                tr[c, pl.ds(pl.multiple_of((f - 1) * rows + r0, 8), 8), :] = val - prev
                prev = val
            tick(t * (n // unroll) + b)
            return state, prev

        lax.fori_loop(0, n // unroll, inner, (state, prev))
        return 0

    lax.fori_loop(0, comps * chunks, outer, 0)


def speed_sweep(sr, ar, n, rows):
    def body(f, _):
        for r0 in range(0, rows, 8):
            ld = lambda i: sr[pl.ds(pl.multiple_of(i * rows + r0, 8), 8), :]
            m = ld(f)
            for o in range(1, 6):
                m = jnp.maximum(m, ld(f + o))
            ar[pl.ds(pl.multiple_of(f * rows + r0, 8), 8), :] = m
        return 0

    lax.fori_loop(0, n + 1, body, 0)


def flux_sweep(qr, gr, sr, first, count, normal):
    def body(i, _):
        at = pl.ds(pl.multiple_of(i * 8, 8), 8)
        g, s = flux_parts([qr[c, at, :] for c in range(6)], normal)
        for c in range(6):
            gr[c, at, :] = g[c]
        sr[at, :] = s
        return 0

    lax.fori_loop(first, first + count, body, 0, unroll=2)


def transpose_in(qx, tq, qy, gy, sy, tick):
    def block(blk, _):
        for c in range(6):
            x = qx[c, pl.ds(pl.multiple_of(96 + blk * 128, 32), 128), :]
            tq[c] = x.T

        def rows(y, _):
            y0 = pl.multiple_of(y * 8, 8)
            q = [tq[c, pl.ds(y0, 8), :] for c in range(6)]
            g, s = flux_parts(q, 2)
            base = (3 + y0) * 8
            for c in range(6):
                spot = pl.ds(base + (c % 2) * 4 + blk, 8, stride=8)
                qy[c // 2, spot, :] = q[c]
                gy[c // 2, spot, :] = g[c]
            sy[pl.ds(base + blk, 8, stride=8), :] = s
            sy[pl.ds(base + 4 + blk, 8, stride=8), :] = s
            return 0

        lax.fori_loop(0, 16, rows, 0)
        r, m1, m2, m3, en, ev = [tq[c, 0:8, :] for c in range(6)]
        rinv = 1.0 / r
        ke = (m1 * m1 + m2 * m2 + m3 * m3) * (0.5 * rinv)
        temp = (en - ke - ev) * (1.0 / 2.5) * rinv
        ghost = [r, -m1, -m2, -m3, en - 2.5 * r * (temp - 0.36 / temp), ev]
        g, s = flux_parts(ghost, 2)
        for k in range(3):
            for c in range(6):
                spot = pl.ds((2 - k) * 8 + (c % 2) * 4 + blk, 1)
                qy[c // 2, spot, :] = ghost[c][k : k + 1]
                gy[c // 2, spot, :] = g[c][k : k + 1]
            sy[pl.ds((2 - k) * 8 + blk, 1), :] = s[k : k + 1]
            sy[pl.ds((2 - k) * 8 + 4 + blk, 1), :] = s[k : k + 1]
        tick(blk)
        return 0

    lax.fori_loop(0, 4, block, 0)
    for k in range(3):
        src, dst = pl.ds(130 * 8, 8), pl.ds((131 + k) * 8, 8)
        for c in range(3):
            qy[c, dst, :] = qy[c, src, :]
            gy[c, dst, :] = gy[c, src, :]
        sy[dst, :] = sy[src, :]


def swap_in(qx, qz):
    def body(z, _):
        for c in range(6):
            for x0 in (0, 8):
                v = qx[c, pl.ds((3 + x0) * 32 + z, 8, stride=32), :]
                qz[c, pl.ds(pl.multiple_of((3 + z) * 16 + x0, 8), 8), :] = v
        return 0

    lax.fori_loop(0, 32, body, 0)


def combine(qx, tx, tz, ty, out, strength):
    def block(blk, _):
        for c in range(6):
            t = ty[c // 2, pl.ds((c % 2) * 4 + blk, 128, stride=8), :].T
            for k in range(4):
                x = blk * 4 + k
                span = tz[c, pl.ds(x, 32, stride=16), :]
                at = pl.ds(pl.multiple_of(x * 32, 32), 32)
                q = qx[c, pl.ds(pl.multiple_of(96 + x * 32, 32), 32), :]
                rate = tx[c, at, :] + span + t[k * 32 : k * 32 + 32] + strength(x) * q
                out[c, at, :] = q - 0.05 * rate
        return 0

    lax.fori_loop(0, 4, block, 0)

    def relax(i, _):
        at = pl.ds(pl.multiple_of(96 + i * 8, 8), 8)
        r, m1, m2, m3, en, ev = [qx[c, at, :] for c in range(6)]
        rinv = 1.0 / r
        ke = (m1 * m1 + m2 * m2 + m3 * m3) * (0.5 * rinv)
        p = (en - ke - ev) * (1.0 / 2.5)
        temp = p * rinv
        eq = 2.0 / (jnp.exp(2.0 / temp) - 1.0)
        tau = 0.5 * jnp.exp(1.5 * (jnp.exp(jnp.log(temp) * (-1.0 / 3.0)) - 1.0))
        dst = pl.ds(pl.multiple_of(i * 8, 8), 8)
        out[5, dst, :] = out[5, dst, :] + 0.05 * ((r * eq - ev) * p / tau)
        return 0

    lax.fori_loop(0, 64, relax, 0, unroll=2)


def weno_scratch():
    v = lambda *s: pltpu.VMEM(s, F32)
    return dict(
        qx=v(6, 22 * 32, 128), gx=v(6, 22 * 32, 128), sx=v(22 * 32, 128), ax=v(17 * 32, 128), tx=v(6, 16 * 32, 128),
        qz=v(6, 38 * 16, 128), gz=v(6, 38 * 16, 128), sz=v(38 * 16, 128), az=v(33 * 16, 128), tz=v(6, 32 * 16, 128),
        tq=v(6, 128, 128), qy=v(3, 134 * 8, 128), gy=v(3, 134 * 8, 128), sy=v(134 * 8, 128), ay=v(129 * 8, 128), ty=v(3, 128 * 8, 128),
    )


MESH = pl.DeviceIdType.MESH
PLANES = 25
STEP = 2
HOP = 9
PIECES = 24
AHEAD = 2
WIRE_TICKS = PIECES * STEP + 8 * HOP


def spectral_kernel(coeff, table, wave, out, acc):
    step = pl.program_id(0)

    @pl.when(step == 0)
    def _():
        acc[...] = jnp.zeros_like(acc)

    iota = lambda shape, d: lax.broadcasted_iota(jnp.int32, shape, d)
    rows = jnp.where(iota((224, 32), 0) // 8 == iota((224, 32), 1), 1.0, 0.0).astype(jnp.bfloat16)
    col = iota((32, 256), 1)
    cols = jnp.where(col // 128 * 16 + col % 128 // 8 == iota((32, 256), 0), 1.0, 0.0).astype(jnp.bfloat16)
    wide = jnp.dot(wave[0], cols, preferred_element_type=F32).astype(jnp.bfloat16)
    wide = jnp.dot(rows, wide, preferred_element_type=F32)
    kron = jnp.where(iota((224, 256), 0) % 8 == iota((224, 256), 1) % 8, wide, 0.0).astype(jnp.bfloat16)
    both = jnp.concatenate([coeff[0], coeff[1]], axis=1)
    for half in range(2):
        lanes = slice(half * 256, half * 256 + 256)
        re = jnp.dot(both, table[:, half * 256 : half * 256 + 256], preferred_element_type=F32)
        im = jnp.dot(both, table[:, 512 + half * 256 : 768 + half * 256], preferred_element_type=F32)
        re = re.reshape(16, 6, 8, 256)
        im = im.reshape(16, 6, 8, 256)
        for v in range(6):
            modes = jnp.concatenate([re[:, v].reshape(128, 256), im[:, v].reshape(128, 256)], axis=0)
            acc[v, :, lanes] += jnp.dot(kron, modes.astype(jnp.bfloat16), preferred_element_type=F32)

    @pl.when(step == pl.num_programs(0) - 1)
    def _():
        lane = lax.broadcasted_iota(jnp.int32, (8, 128), 1)
        low64 = lane < 64
        low32 = lane % 64 < 32

        def tiles(t, _):
            v, g = t // 7, t % 7
            gz = lax.axis_index("gz")
            for jb in range(4):
                f = [acc[v, pl.ds(pl.multiple_of(g * 32 + i * 8, 8), 8), jb * 128 : jb * 128 + 128] for i in range(4)]
                n0 = jnp.where(low64, f[0], pltpu.roll(f[2], 64, 1))
                n2 = jnp.where(low64, pltpu.roll(f[0], 64, 1), f[2])
                n1 = jnp.where(low64, f[1], pltpu.roll(f[3], 64, 1))
                n3 = jnp.where(low64, pltpu.roll(f[1], 64, 1), f[3])
                for k, (a, b) in enumerate(((n0, n1), (n2, n3))):
                    out[v, (4 * jb + 2 * k + 16 - gz) % 16, g] = jnp.where(low32, a, pltpu.roll(b, 32, 1))
                    out[v, (4 * jb + 2 * k + 17 - gz) % 16, g] = jnp.where(low32, pltpu.roll(a, 96, 1), b)
            return 0

        lax.fori_loop(0, 42, tiles, 0, unroll=6)


def spectral(coeff, feed_plane):
    n = np.arange(512)
    angle = 2.0 * np.pi / 512.0 * ((n[:, None] * n[None, :]) % 512)
    cz, sz = np.cos(angle), np.sin(angle)
    table = jnp.asarray(np.block([[cz, sz], [-sz, cz]]).astype(np.float32)).astype(jnp.bfloat16)
    shape = (4, 32, 32)
    step, plane, col = (lax.broadcasted_iota(jnp.int32, shape, d) for d in range(3))
    feed = jnp.pad(feed_plane, (0, 32 - PLANES)).reshape(1, 32, 1)
    mode = lax.axis_index("gx") * 64 + step * 16 + col % 16
    ids = (feed * mode + 512 * (col // 16)) % 2048
    wave = jnp.cos(2.0 * math.pi / 2048 * ids.astype(F32))
    wave = jnp.where(plane < PLANES, wave, 0.0).astype(jnp.bfloat16)
    return pl.pallas_call(
        spectral_kernel,
        grid=(4,),
        out_shape=jax.ShapeDtypeStruct((6, 16, 7, 8, 128), F32),
        in_specs=[
            pl.BlockSpec((2, 768, 512), lambda i: (0, i, 0)),
            pl.BlockSpec((1024, 1024), lambda i: (0, 0)),
            pl.BlockSpec((1, 32, 32), lambda i: (i, 0, 0)),
        ],
        out_specs=pl.BlockSpec((6, 16, 7, 8, 128), lambda i: (0, 0, 0, 0, 0)),
        scratch_shapes=[pltpu.VMEM((6, 224, 512), F32)],
        compiler_params=pltpu.CompilerParams(dimension_semantics=("arbitrary",), vmem_limit_bytes=56 * 2**20),
    )(coeff.reshape(2, 3072, 512), table, wave)


def main_kernel(names, q_hbm, part, out, *scratch):
    s = dict(zip(names, scratch))
    qx, qz, land, swap, feed = s["qx"], s["qz"], s["land"], s["swap"], s["feed"]
    gx, gz = lax.axis_index("gx"), lax.axis_index("gz")
    z, xlo = gx % 8, gx // 8
    z_next = {0: xlo * 8 + (z + 1) % 8, 1: xlo * 8 + (z + 7) % 8}
    is_root = z < 2

    load = pltpu.make_async_copy(q_hbm, qx.at[:, 96:608], s["load_sem"])
    load.start()

    barrier = pltpu.get_barrier_semaphore()

    def greet(a, b):
        pl.semaphore_signal(barrier, inc=1, device_id=(a, b), device_id_type=MESH)

    @pl.when(gx < 15)
    def _():
        greet(gx + 1, gz)

    @pl.when(gx > 0)
    def _():
        greet(gx - 1, gz)

    greet((gx + 8) % 16, gz)
    greet(z_next[0], gz)
    greet(z_next[1], gz)
    greet(gx, (gz + 1) % 16)
    greet(gx, (gz + 15) % 16)

    @pl.when(is_root)
    def _():
        def each(b, _):
            @pl.when((xlo == 1) | (b != gz))
            def _():
                greet(z, b)

            @pl.when(xlo == 0)
            def _():
                greet(8 + z, b)

            return 0

        lax.fori_loop(0, 16, each, 0)

    ends = jnp.where((gx == 0) | (gx == 15), 1, 0)
    roots = jnp.where(is_root, jnp.where(xlo == 0, 31, 16), 0)
    pl.semaphore_wait(barrier, 7 - ends + roots)

    def remote(src, dst, ssem, rsem, a, b):
        return pltpu.make_async_remote_copy(
            src_ref=src, dst_ref=dst, send_sem=ssem, recv_sem=rsem, device_id=(a, b), device_id_type=MESH
        )

    groups = (slice(0, 4), slice(4, 7))
    every = slice(0, 7)
    lines = ((0, (z + 7) % 8), (1, (8 - z) % 8))

    def exchange(d, i):
        block = (i // 2, pl.ds(8 * d + i % 2 * 4, 4))
        return remote(part.at[1 - xlo, *block], swap.at[block], s["swap_send"], s["swap_recv"].at[d, i], (gx + 8) % 16, gz)

    def tick(n):
        for d, pos in lines:
            first, second = groups[d], groups[1 - d]

            def turn(k, last):
                v, e = k // 8, 8 * d + k % 8
                held = lambda g: land.at[v, e, g]
                mine = lambda g: part[xlo, v, e, g] + swap[v, e, g]
                ssem, rsem = s["send_sem"].at[d], s["recv_sem"].at[d, k]
                onward = lambda g: remote(held(g), held(g), ssem, rsem, z_next[d], gz)

                def add(g):
                    held(g)[...] = held(g)[...] + mine(g)

                def deliver(r):
                    c = (gz + e) % 16
                    place = feed.at[3 * xlo + v, gz, 0 : 4 - r]
                    here = (xlo == 0) & (c == gz)

                    @pl.when(here)
                    def _():
                        pltpu.make_async_copy(held(groups[r]), place, s["feed_sem"]).start()

                    @pl.when(jnp.logical_not(here))
                    def _():
                        remote(held(groups[r]), place, ssem, s["feed_sem"], r, c).start()

                if last:
                    onward(second).wait_recv()
                    add(second)
                    deliver(1 - d)
                    return

                @pl.when(k % 4 == 0)
                def _():
                    exchange(d, k // 4).wait_recv()

                    @pl.when(k < PIECES - 4 * AHEAD)
                    def _():
                        exchange(d, k // 4 + AHEAD).start()

                @pl.when(pos == 0)
                def _():
                    held(first)[...] = mine(first)
                    onward(first).start()

                @pl.when(pos == 1)
                def _():
                    held(second)[...] = mine(second)
                    onward(first).wait_recv()
                    add(first)
                    onward(every).start()

                @pl.when((pos > 1) & (pos < 7))
                def _():
                    onward(every).wait_recv()
                    add(every)
                    onward(every).start()

                @pl.when(pos == 7)
                def _():
                    onward(every).wait_recv()
                    add(every)
                    onward(second).start()
                    deliver(d)

            def due(place, ok, last):
                m = n - place * HOP
                pl.when(ok & (m >= 0) & (m < PIECES * STEP) & (m % STEP == 0))(lambda: turn(m // STEP, last))

            due(pos, pos >= 0, False)
            due(8, pos == 0, True)

    halo = []
    for i, (src, dst, a, b, ok_send, ok_recv) in enumerate(
        (
            (qx.at[:, 512:608], qx.at[:, 0:96], jnp.minimum(gx + 1, 15), gz, gx < 15, gx > 0),
            (qx.at[:, 96:192], qx.at[:, 608:704], jnp.maximum(gx - 1, 0), gz, gx > 0, gx < 15),
            (qz.at[:, 512:560], qz.at[:, 0:48], gx, (gz + 1) % 16, None, None),
            (qz.at[:, 48:96], qz.at[:, 560:608], gx, (gz + 15) % 16, None, None),
        )
    ):
        halo.append((remote(src, dst, s["halo_send"].at[i], s["halo_recv"].at[i], a, b), ok_send, ok_recv))

    def on(ok, act):
        if ok is None:
            act()
        else:
            pl.when(ok)(act)

    def exchanges(i, _):
        exchange(0, i).start()
        exchange(1, i).start()
        return 0

    lax.fori_loop(0, AHEAD, exchanges, 0)
    load.wait()
    for copy, ok, _ in halo[:2]:
        on(ok, copy.start)
    swap_in(qx, qz)
    for copy, ok, _ in halo[2:]:
        on(ok, copy.start)
    transpose_in(qx, s["tq"], s["qy"], s["gy"], s["sy"], lambda blk: tick(blk))
    speed_sweep(s["sy"], s["ay"], 128, 8)
    face_sweep(s["qy"], s["gy"], s["ay"], s["ty"], 3, 128, 8, 8, lambda i: tick(i + 4))
    for copy, _, ok in halo[2:]:
        on(ok, copy.wait_recv)
    flux_sweep(qz, s["gz"], s["sz"], 0, 76, 3)
    speed_sweep(s["sz"], s["az"], 32, 16)
    face_sweep(qz, s["gz"], s["az"], s["tz"], 6, 32, 16, 8, lambda i: tick(i + 52))
    for copy, _, ok in halo[:2]:
        on(ok, copy.wait_recv)

    @pl.when(gx == 0)
    def _():
        for i in range(3):
            qx[:, i * 32 : i * 32 + 32] = qx[:, 96:128]

    @pl.when(gx == 15)
    def _():
        for i in range(3):
            qx[:, 608 + i * 32 : 640 + i * 32] = qx[:, 576:608]

    flux_sweep(qx, s["gx"], s["sx"], 0, 88, 1)
    speed_sweep(s["sx"], s["ax"], 16, 32)
    face_sweep(qx, s["gx"], s["ax"], s["tx"], 6, 16, 32, 16, lambda i: tick(i + 100))

    def strength(x):
        plane = gx * 16 + x
        level = 1.0 - plane.astype(F32) * (1.0 / PLANES)
        return jnp.where(plane < PLANES, 2.0 * level * level, 0.0)

    combine(qx, s["tx"], s["tz"], s["ty"], out, strength)

    def drain(n, _):
        tick(n)
        return 0

    lax.fori_loop(124, WIRE_TICKS, drain, 0)

    for r in range(2):

        @pl.when(gx == r)
        def _():
            count = 4 if r == 0 else 3
            whole = feed.at[:, :, 0:count]
            pltpu.make_async_copy(whole, whole, s["feed_sem"]).wait()

            def add(v, _):
                for g in range(count):
                    t = feed[v, :, g].reshape(128, 128).T
                    for i in range(4):
                        x = g * 4 + i
                        at = slice(x * 32, x * 32 + 32)
                        out[v, at, :] = out[v, at, :] + (0.05 * strength(jnp.int32(x))) * t[i * 32 : i * 32 + 32]
                return 0

            lax.fori_loop(0, 6, add, 0)

    for copy, ok, _ in halo:
        on(ok, copy.wait_send)
    pltpu.make_async_copy(swap, swap, s["swap_send"]).wait()
    for d, pos in lines:

        def sent(blocks, g):
            span = land.at[:, blocks, g]
            pltpu.make_async_copy(span, span, s["send_sem"].at[d]).wait()

        if d == 1:
            sent(slice(0, 8), every)
        else:
            sent(slice(0, 7), every)
            own = xlo == 0
            pl.when(own & (pos == 0))(lambda: sent(slice(7, 8), groups[0]))
            pl.when(own & (pos == 7))(lambda: sent(slice(7, 8), groups[1]))
            pl.when(jnp.logical_not(own) | ((pos > 0) & (pos < 7)))(lambda: sent(slice(7, 8), every))


def local(conserved_fields, coeff, feed_plane):
    part = spectral(coeff, feed_plane)
    scratch = weno_scratch()
    scratch.update(
        land=pltpu.VMEM((3, 16, 7, 8, 128), F32),
        swap=pltpu.VMEM((3, 16, 7, 8, 128), F32),
        feed=pltpu.VMEM((6, 16, 4, 8, 128), F32),
        load_sem=pltpu.SemaphoreType.DMA,
        halo_send=pltpu.SemaphoreType.DMA((4,)),
        halo_recv=pltpu.SemaphoreType.DMA((4,)),
        send_sem=pltpu.SemaphoreType.DMA((2,)),
        recv_sem=pltpu.SemaphoreType.DMA((2, PIECES)),
        swap_send=pltpu.SemaphoreType.DMA,
        swap_recv=pltpu.SemaphoreType.DMA((2, 6)),
        feed_sem=pltpu.SemaphoreType.DMA,
    )
    names = list(scratch)
    out = pl.pallas_call(
        lambda *refs: main_kernel(names, *refs),
        out_shape=jax.ShapeDtypeStruct((6, 512, 128), F32),
        in_specs=[pl.BlockSpec(memory_space=pl.ANY), pl.BlockSpec(memory_space=pltpu.VMEM)],
        out_specs=pl.BlockSpec(memory_space=pltpu.VMEM),
        scratch_shapes=list(scratch.values()),
        compiler_params=pltpu.CompilerParams(collective_id=0, has_side_effects=True, vmem_limit_bytes=56 * 2**20),
        name="section",
    )(conserved_fields.reshape(6, 512, 128), part.reshape(2, 3, 16, 7, 8, 128))
    return out.reshape(6, 16, 32, 128)


def solution(mesh):
    placed = (P(None, "gx", "gz", None), P(None, "gx", None, "gz", None), P())
    return jax.shard_map(
        local, mesh=mesh, in_specs=placed, out_specs=P(None, "gx", "gz", None), check_vma=False
    )
```

```python
import math

import jax, jax.numpy as jnp
from jax import lax
from jax.experimental import pallas as pl
from jax.experimental.pallas import tpu as pltpu
from jax.sharding import PartitionSpec as P
import numpy as np

F32 = jnp.float32
NXL, NZL, NYL = 16, 32, 128


def flux_parts(q, n):
    r, m1, m2, m3, en, ev = q
    rinv = 1.0 / r
    un = q[n] * rinv
    ke = (m1 * m1 + m2 * m2 + m3 * m3) * (0.5 * rinv)
    p = (en - ke - ev) * (1.0 / 2.5)
    s = jnp.abs(un) + jnp.sqrt(1.4 * (p * rinv))
    h = 0.5 * un
    g = [q[c] * h for c in range(6)]
    g[n] = g[n] + 0.5 * p
    g[4] = g[4] + p * h
    return g, 0.5 * s


def ratio(num, den):
    return num * pl.reciprocal(den, approx=False)


def correction(d2, d3, e0, e1, e2):
    d2s = d2 * d2 + 1e-6
    b0 = d2s + e0 * (d2 + (4.0 / 3.0) * e0)
    b1 = d2s + e1 * (d2 + (4.0 / 3.0) * e1)
    b2 = (d3 * d3 + 1e-6) + e2 * ((4.0 / 3.0) * e2 - d3)
    p0, p1, p2 = b0 * b0, b1 * b1, b2 * b2
    w0 = p1 * p2
    w1 = 6.0 * (p0 * p2)
    w2 = 3.0 * (p0 * p1)
    num = e0 * w0 + e1 * w1 + (e1 + 0.5 * (e1 - e2)) * w2
    return ratio(num, w0 + w1 + w2)


def face_value(a, gs, dg, dq, eg, eq):
    ad = [a * x for x in dq]
    ae = [a * x for x in eq]
    pd2, pd3 = dg[0] + ad[0], dg[1] + ad[1]
    md2, md3 = ad[2] - dg[2], ad[1] - dg[1]
    pe = [eg[i] + ae[i] for i in (0, 1, 2)]
    me = [eg[i] - ae[i] for i in (3, 2, 1)]
    lead = (gs - ad[1]) + 0.5 * (pd2 + md2)
    return lead + (1.0 / 3.0) * (correction(pd2, pd3, *pe) + correction(md2, md3, *me))


def face_sweep(qr, gr, ar, tr, comps, n, rows, unroll, tick):
    chunks = rows // 8

    def outer(t, _):
        c = t // chunks
        r0 = (t % chunks) * 8
        at = lambda ref, i: ref[c, pl.ds(pl.multiple_of(i * rows + r0, 8), 8), :]

        def advance(state, f):
            dq, dg, eq, eg = state
            dqn = at(qr, f + 5) - at(qr, f + 4)
            dgn = at(gr, f + 5) - at(gr, f + 4)
            eqn, egn = dqn - dq[2], dgn - dg[2]
            return (dq[0], dq[1], dq[2], dqn), (dg[0], dg[1], dg[2], dgn), (*eq, eqn), (*eg, egn)

        def one(state, f):
            dq, dg, eq, eg = advance(state, f)
            a = ar[pl.ds(pl.multiple_of(f * rows + r0, 8), 8), :]
            gs = at(gr, f + 2) + at(gr, f + 3)
            val = face_value(a, gs, dg[:3], dq[:3], eg, eq)
            return (dq[1:], dg[1:], eq[1:], eg[1:]), val

        qs = [at(qr, i) for i in range(5)]
        gs = [at(gr, i) for i in range(5)]
        dq = [qs[i + 1] - qs[i] for i in range(4)]
        dg = [gs[i + 1] - gs[i] for i in range(4)]
        eq = [dq[i + 1] - dq[i] for i in range(3)]
        eg = [dg[i + 1] - dg[i] for i in range(3)]
        state = (tuple(dq[1:]), tuple(dg[1:]), tuple(eq), tuple(eg))
        state, prev = one(state, 0)

        def inner(b, carry):
            state, prev = carry
            for k in range(unroll):
                f = b * unroll + k + 1
                state, val = one(state, f)
                tr[c, pl.ds(pl.multiple_of((f - 1) * rows + r0, 8), 8), :] = val - prev
                prev = val
            tick(t * (n // unroll) + b)
            return state, prev

        lax.fori_loop(0, n // unroll, inner, (state, prev))
        return 0

    lax.fori_loop(0, comps * chunks, outer, 0)


def speed_sweep(sr, ar, n, rows):
    def body(f, _):
        for r0 in range(0, rows, 8):
            ld = lambda i: sr[pl.ds(pl.multiple_of(i * rows + r0, 8), 8), :]
            m = ld(f)
            for o in range(1, 6):
                m = jnp.maximum(m, ld(f + o))
            ar[pl.ds(pl.multiple_of(f * rows + r0, 8), 8), :] = m
        return 0

    lax.fori_loop(0, n + 1, body, 0)


def flux_sweep(qr, gr, sr, first, count, normal):
    def body(i, _):
        at = pl.ds(pl.multiple_of(i * 8, 8), 8)
        g, s = flux_parts([qr[c, at, :] for c in range(6)], normal)
        for c in range(6):
            gr[c, at, :] = g[c]
        sr[at, :] = s
        return 0

    lax.fori_loop(first, first + count, body, 0, unroll=2)


def transpose_in(qx, tq, qy, gy, sy, tick):
    def block(blk, _):
        for c in range(6):
            x = qx[c, pl.ds(pl.multiple_of(96 + blk * 128, 32), 128), :]
            tq[c] = x.T

        def rows(y, _):
            y0 = pl.multiple_of(y * 8, 8)
            q = [tq[c, pl.ds(y0, 8), :] for c in range(6)]
            g, s = flux_parts(q, 2)
            base = (3 + y0) * 8
            for c in range(6):
                spot = pl.ds(base + (c % 2) * 4 + blk, 8, stride=8)
                qy[c // 2, spot, :] = q[c]
                gy[c // 2, spot, :] = g[c]
            sy[pl.ds(base + blk, 8, stride=8), :] = s
            sy[pl.ds(base + 4 + blk, 8, stride=8), :] = s
            return 0

        lax.fori_loop(0, 16, rows, 0)
        r, m1, m2, m3, en, ev = [tq[c, 0:8, :] for c in range(6)]
        rinv = 1.0 / r
        ke = (m1 * m1 + m2 * m2 + m3 * m3) * (0.5 * rinv)
        temp = (en - ke - ev) * (1.0 / 2.5) * rinv
        ghost = [r, -m1, -m2, -m3, en - 2.5 * r * (temp - 0.36 / temp), ev]
        g, s = flux_parts(ghost, 2)
        for k in range(3):
            for c in range(6):
                spot = pl.ds((2 - k) * 8 + (c % 2) * 4 + blk, 1)
                qy[c // 2, spot, :] = ghost[c][k : k + 1]
                gy[c // 2, spot, :] = g[c][k : k + 1]
            sy[pl.ds((2 - k) * 8 + blk, 1), :] = s[k : k + 1]
            sy[pl.ds((2 - k) * 8 + 4 + blk, 1), :] = s[k : k + 1]
        tick(blk)
        return 0

    lax.fori_loop(0, 4, block, 0)
    for k in range(3):
        src, dst = pl.ds(130 * 8, 8), pl.ds((131 + k) * 8, 8)
        for c in range(3):
            qy[c, dst, :] = qy[c, src, :]
            gy[c, dst, :] = gy[c, src, :]
        sy[dst, :] = sy[src, :]


def swap_in(qx, qz):
    def body(z, _):
        for c in range(6):
            for x0 in (0, 8):
                v = qx[c, pl.ds((3 + x0) * 32 + z, 8, stride=32), :]
                qz[c, pl.ds(pl.multiple_of((3 + z) * 16 + x0, 8), 8), :] = v
        return 0

    lax.fori_loop(0, 32, body, 0)


def combine(qx, tx, tz, ty, out, strength):
    def block(blk, _):
        for c in range(6):
            t = ty[c // 2, pl.ds((c % 2) * 4 + blk, 128, stride=8), :].T
            for k in range(4):
                x = blk * 4 + k
                span = tz[c, pl.ds(x, 32, stride=16), :]
                at = pl.ds(pl.multiple_of(x * 32, 32), 32)
                q = qx[c, pl.ds(pl.multiple_of(96 + x * 32, 32), 32), :]
                rate = tx[c, at, :] + span + t[k * 32 : k * 32 + 32] + strength(x) * q
                out[c, at, :] = q - 0.05 * rate
        return 0

    lax.fori_loop(0, 4, block, 0)

    def relax(i, _):
        at = pl.ds(pl.multiple_of(96 + i * 8, 8), 8)
        r, m1, m2, m3, en, ev = [qx[c, at, :] for c in range(6)]
        rinv = 1.0 / r
        ke = (m1 * m1 + m2 * m2 + m3 * m3) * (0.5 * rinv)
        p = (en - ke - ev) * (1.0 / 2.5)
        temp = p * rinv
        eq = 2.0 / (jnp.exp(2.0 / temp) - 1.0)
        tau = 0.5 * jnp.exp(1.5 * (jnp.exp(jnp.log(temp) * (-1.0 / 3.0)) - 1.0))
        dst = pl.ds(pl.multiple_of(i * 8, 8), 8)
        out[5, dst, :] = out[5, dst, :] + 0.05 * ((r * eq - ev) * p / tau)
        return 0

    lax.fori_loop(0, 64, relax, 0, unroll=2)


def weno_scratch():
    v = lambda *s: pltpu.VMEM(s, F32)
    return dict(
        qx=v(6, 22 * 32, 128), gx=v(6, 22 * 32, 128), sx=v(22 * 32, 128), ax=v(17 * 32, 128), tx=v(6, 16 * 32, 128),
        qz=v(6, 38 * 16, 128), gz=v(6, 38 * 16, 128), sz=v(38 * 16, 128), az=v(33 * 16, 128), tz=v(6, 32 * 16, 128),
        tq=v(6, 128, 128), qy=v(3, 134 * 8, 128), gy=v(3, 134 * 8, 128), sy=v(134 * 8, 128), ay=v(129 * 8, 128), ty=v(3, 128 * 8, 128),
    )


MESH = pl.DeviceIdType.MESH
PLANES = 25
STEP = 2
HOP = 11
PIECES = 24
WIRE_TICKS = PIECES * STEP + 8 * HOP


def kron_table(wave, kron):
    iota = lambda shape, d: lax.broadcasted_iota(jnp.int32, shape, d)
    rows = jnp.where(iota((224, 32), 0) // 8 == iota((224, 32), 1), 1.0, 0.0).astype(jnp.bfloat16)
    col = iota((128, 1024), 1)
    cols = jnp.where(col // 512 * 64 + col % 512 // 8 == iota((128, 1024), 0), 1.0, 0.0).astype(jnp.bfloat16)
    wide = jnp.dot(wave[...], cols, preferred_element_type=F32).astype(jnp.bfloat16)
    wide = jnp.dot(rows, wide, preferred_element_type=F32)
    kron[...] = jnp.where(iota((224, 1024), 0) % 8 == iota((224, 1024), 1) % 8, wide, 0.0).astype(jnp.bfloat16)


def spectral(i, raw, rows, table, kron, modes, sums, put, tick):
    for p in range(2):
        rows[:, p * 512 : p * 512 + 512] = raw[i % 2, p].reshape(512, 512)
    for h in range(2):
        for p in range(2):
            at = p * 512 + h * 256
            span = jnp.dot(rows[...], table[:, at : at + 256], preferred_element_type=F32)
            modes[p * 512 : p * 512 + 512, :] = span.astype(jnp.bfloat16)
            tick(h * 3 + p)
        sums[:, h * 256 : h * 256 + 256] = jnp.dot(kron[...], modes[...], preferred_element_type=F32)
        tick(h * 3 + 2)
    lane = lax.broadcasted_iota(jnp.int32, (8, 128), 1)
    low64 = lane < 64
    low32 = lane % 64 < 32
    for g in range(7):
        for jb in range(4):
            f = [sums[g * 32 + n * 8 : g * 32 + n * 8 + 8, jb * 128 : jb * 128 + 128] for n in range(4)]
            n0 = jnp.where(low64, f[0], pltpu.roll(f[2], 64, 1))
            n2 = jnp.where(low64, pltpu.roll(f[0], 64, 1), f[2])
            n1 = jnp.where(low64, f[1], pltpu.roll(f[3], 64, 1))
            n3 = jnp.where(low64, pltpu.roll(f[1], 64, 1), f[3])
            for k, (a, b) in enumerate(((n0, n1), (n2, n3))):
                put(4 * jb + 2 * k, g, jnp.where(low32, a, pltpu.roll(b, 32, 1)))
                put(4 * jb + 2 * k + 1, g, jnp.where(low32, pltpu.roll(a, 96, 1), b))


def tables(feed_plane):
    n = np.arange(512)
    angle = 2.0 * np.pi / 512.0 * ((n[:, None] * n[None, :]) % 512)
    cz, sz = np.cos(angle), np.sin(angle)
    table = jnp.asarray(np.block([[cz, sz], [-sz, cz]]).astype(np.float32)).astype(jnp.bfloat16)
    plane, col = (lax.broadcasted_iota(jnp.int32, (32, 128), d) for d in range(2))
    feed = jnp.pad(feed_plane, (0, 32 - PLANES)).reshape(32, 1)
    mode = lax.axis_index("gx") * 64 + col % 64
    ids = (feed * mode + 512 * (col // 64)) % 2048
    wave = jnp.cos(2.0 * math.pi / 2048 * ids.astype(F32))
    return table, jnp.where(plane < PLANES, wave, 0.0).astype(jnp.bfloat16)


def main_kernel(names, q_hbm, coeff, table, wave, out, *scratch):
    s = dict(zip(names, scratch))
    part = s["part"]
    qx, qz, land, swap, feed = s["qx"], s["qz"], s["land"], s["swap"], s["feed"]
    gx, gz = lax.axis_index("gx"), lax.axis_index("gz")
    z, xlo = gx % 8, gx // 8
    z_next = {0: xlo * 8 + (z + 1) % 8, 1: xlo * 8 + (z + 7) % 8}
    is_root = z < 2

    load = pltpu.make_async_copy(q_hbm, qx.at[:, 96:608], s["load_sem"])
    load.start()

    def fetch(i):
        v = jnp.where(i < 3, 3 - 3 * xlo, 3 * xlo) + i % 3
        return pltpu.make_async_copy(coeff.at[:, :, v], s["raw"].at[i % 2], s["raw_sem"].at[i % 2])

    fetch(0).start()
    fetch(1).start()
    kron_table(wave, s["kron"])

    barrier = pltpu.get_barrier_semaphore()

    def greet(a, b):
        pl.semaphore_signal(barrier, inc=1, device_id=(a, b), device_id_type=MESH)

    @pl.when(gx < 15)
    def _():
        greet(gx + 1, gz)

    @pl.when(gx > 0)
    def _():
        greet(gx - 1, gz)

    greet((gx + 8) % 16, gz)
    greet(z_next[0], gz)
    greet(z_next[1], gz)
    greet(gx, (gz + 1) % 16)
    greet(gx, (gz + 15) % 16)

    @pl.when(is_root)
    def _():
        def each(b, _):
            @pl.when((xlo == 1) | (b != gz))
            def _():
                greet(z, b)

            @pl.when(xlo == 0)
            def _():
                greet(8 + z, b)

            return 0

        lax.fori_loop(0, 16, each, 0)

    ends = jnp.where((gx == 0) | (gx == 15), 1, 0)
    roots = jnp.where(is_root, jnp.where(xlo == 0, 31, 16), 0)
    pl.semaphore_wait(barrier, 7 - ends + roots)

    def remote(src, dst, ssem, rsem, a, b):
        return pltpu.make_async_remote_copy(
            src_ref=src, dst_ref=dst, send_sem=ssem, recv_sem=rsem, device_id=(a, b), device_id_type=MESH
        )

    groups = (slice(0, 4), slice(4, 7))
    every = slice(0, 7)
    lines = ((0, (z + 7) % 8), (1, (8 - z) % 8))

    def exchange(d, i):
        block = (i // 2, pl.ds(8 * d + i % 2 * 4, 4))
        return remote(part.at[1 - xlo, *block], swap.at[block], s["swap_send"], s["swap_recv"].at[d, i], (gx + 8) % 16, gz)

    def tick(n):
        for d, pos in lines:
            first, second = groups[d], groups[1 - d]

            def turn(k, last):
                v, e = k // 8, 8 * d + k % 8
                held = lambda g: land.at[v, e, g]
                mine = lambda g: part[xlo, v, e, g] + swap[v, e, g]
                ssem, rsem = s["send_sem"].at[d], s["recv_sem"].at[d, k]
                onward = lambda g: remote(held(g), held(g), ssem, rsem, z_next[d], gz)

                def add(g):
                    held(g)[...] = held(g)[...] + mine(g)

                def deliver(r):
                    c = (gz + e) % 16
                    place = feed.at[3 * xlo + v, gz, 0 : 4 - r]
                    here = (xlo == 0) & (c == gz)

                    @pl.when(here)
                    def _():
                        pltpu.make_async_copy(held(groups[r]), place, s["feed_sem"]).start()

                    @pl.when(jnp.logical_not(here))
                    def _():
                        remote(held(groups[r]), place, ssem, s["feed_sem"], r, c).start()

                if last:
                    onward(second).wait_recv()
                    add(second)
                    deliver(1 - d)
                    return

                @pl.when(k % 4 == 0)
                def _():
                    exchange(d, k // 4).wait_recv()

                @pl.when(pos == 0)
                def _():
                    held(first)[...] = mine(first)
                    onward(first).start()

                @pl.when(pos == 1)
                def _():
                    held(second)[...] = mine(second)
                    onward(first).wait_recv()
                    add(first)
                    onward(every).start()

                @pl.when((pos > 1) & (pos < 7))
                def _():
                    onward(every).wait_recv()
                    add(every)
                    onward(every).start()

                @pl.when(pos == 7)
                def _():
                    onward(every).wait_recv()
                    add(every)
                    onward(second).start()
                    deliver(d)

            def due(place, ok, last):
                m = n - place * HOP
                pl.when(ok & (m >= 0) & (m < PIECES * STEP) & (m % STEP == 0))(lambda: turn(m // STEP, last))

            due(pos, pos >= 0, False)
            due(8, pos == 0, True)

    halo = []
    for i, (src, dst, a, b, ok_send, ok_recv) in enumerate(
        (
            (qx.at[:, 512:608], qx.at[:, 0:96], jnp.minimum(gx + 1, 15), gz, gx < 15, gx > 0),
            (qx.at[:, 96:192], qx.at[:, 608:704], jnp.maximum(gx - 1, 0), gz, gx > 0, gx < 15),
            (qz.at[:, 512:560], qz.at[:, 0:48], gx, (gz + 1) % 16, None, None),
            (qz.at[:, 48:96], qz.at[:, 560:608], gx, (gz + 15) % 16, None, None),
        )
    ):
        halo.append((remote(src, dst, s["halo_send"].at[i], s["halo_recv"].at[i], a, b), ok_send, ok_recv))

    def on(ok, act):
        if ok is None:
            act()
        else:
            pl.when(ok)(act)

    load.wait()
    for copy, ok, _ in halo[:2]:
        on(ok, copy.start)
    swap_in(qx, qz)
    for copy, ok, _ in halo[2:]:
        on(ok, copy.start)

    def variable(i, _):
        half = jnp.where(i < 3, 1 - xlo, xlo)
        fetch(i).wait()

        def put(c, g, tile):
            part[half, i % 3, (c + 16 - gz) % 16, g] = tile

        spectral(i, s["raw"], s["rows"], table, s["kron"], s["modes"], s["sums"], put, lambda j: tick((i - 4) * 6 + j))

        @pl.when(i < 4)
        def _():
            fetch(i + 2).start()

        @pl.when(i < 3)
        def _():
            for h in range(2):
                for d in range(2):
                    exchange(d, i * 2 + h).start()

        return 0

    lax.fori_loop(0, 6, variable, 0)
    transpose_in(qx, s["tq"], s["qy"], s["gy"], s["sy"], lambda blk: tick(blk + 12))
    speed_sweep(s["sy"], s["ay"], 128, 8)
    face_sweep(s["qy"], s["gy"], s["ay"], s["ty"], 3, 128, 8, 8, lambda i: tick(i + 16))
    for copy, _, ok in halo[2:]:
        on(ok, copy.wait_recv)
    flux_sweep(qz, s["gz"], s["sz"], 0, 76, 3)
    speed_sweep(s["sz"], s["az"], 32, 16)
    face_sweep(qz, s["gz"], s["az"], s["tz"], 6, 32, 16, 8, lambda i: tick(i + 64))
    for copy, _, ok in halo[:2]:
        on(ok, copy.wait_recv)

    @pl.when(gx == 0)
    def _():
        for i in range(3):
            qx[:, i * 32 : i * 32 + 32] = qx[:, 96:128]

    @pl.when(gx == 15)
    def _():
        for i in range(3):
            qx[:, 608 + i * 32 : 640 + i * 32] = qx[:, 576:608]

    flux_sweep(qx, s["gx"], s["sx"], 0, 88, 1)
    speed_sweep(s["sx"], s["ax"], 16, 32)
    face_sweep(qx, s["gx"], s["ax"], s["tx"], 6, 16, 32, 16, lambda i: tick(i + 112))

    def strength(x):
        plane = gx * 16 + x
        level = 1.0 - plane.astype(F32) * (1.0 / PLANES)
        return jnp.where(plane < PLANES, 2.0 * level * level, 0.0)

    combine(qx, s["tx"], s["tz"], s["ty"], out, strength)

    def drain(n, _):
        tick(n)
        return 0

    lax.fori_loop(136, WIRE_TICKS, drain, 0)

    for r in range(2):

        @pl.when(gx == r)
        def _():
            count = 4 if r == 0 else 3
            whole = feed.at[:, :, 0:count]
            pltpu.make_async_copy(whole, whole, s["feed_sem"]).wait()

            def add(v, _):
                for g in range(count):
                    t = feed[v, :, g].reshape(128, 128).T
                    for i in range(4):
                        x = g * 4 + i
                        at = slice(x * 32, x * 32 + 32)
                        out[v, at, :] = out[v, at, :] + (0.05 * strength(jnp.int32(x))) * t[i * 32 : i * 32 + 32]
                return 0

            lax.fori_loop(0, 6, add, 0)

    for copy, ok, _ in halo:
        on(ok, copy.wait_send)
    pltpu.make_async_copy(swap, swap, s["swap_send"]).wait()
    for d, pos in lines:

        def sent(blocks, g):
            span = land.at[:, blocks, g]
            pltpu.make_async_copy(span, span, s["send_sem"].at[d]).wait()

        if d == 1:
            sent(slice(0, 8), every)
        else:
            sent(slice(0, 7), every)
            own = xlo == 0
            pl.when(own & (pos == 0))(lambda: sent(slice(7, 8), groups[0]))
            pl.when(own & (pos == 7))(lambda: sent(slice(7, 8), groups[1]))
            pl.when(jnp.logical_not(own) | ((pos > 0) & (pos < 7)))(lambda: sent(slice(7, 8), every))


def local(conserved_fields, coeff, feed_plane):
    table, wave = tables(feed_plane)
    scratch = weno_scratch()
    scratch.update(
        raw=pltpu.VMEM((2, 2, 64, 8, 512), jnp.bfloat16),
        rows=pltpu.VMEM((512, 1024), jnp.bfloat16),
        kron=pltpu.VMEM((224, 1024), jnp.bfloat16),
        modes=pltpu.VMEM((1024, 256), jnp.bfloat16),
        sums=pltpu.VMEM((224, 512), F32),
        part=pltpu.VMEM((2, 3, 16, 7, 8, 128), F32),
        raw_sem=pltpu.SemaphoreType.DMA((2,)),
        land=pltpu.VMEM((3, 16, 7, 8, 128), F32),
        swap=pltpu.VMEM((3, 16, 7, 8, 128), F32),
        feed=pltpu.VMEM((6, 16, 4, 8, 128), F32),
        load_sem=pltpu.SemaphoreType.DMA,
        halo_send=pltpu.SemaphoreType.DMA((4,)),
        halo_recv=pltpu.SemaphoreType.DMA((4,)),
        send_sem=pltpu.SemaphoreType.DMA((2,)),
        recv_sem=pltpu.SemaphoreType.DMA((2, PIECES)),
        swap_send=pltpu.SemaphoreType.DMA,
        swap_recv=pltpu.SemaphoreType.DMA((2, 6)),
        feed_sem=pltpu.SemaphoreType.DMA,
    )
    names = list(scratch)
    out = pl.pallas_call(
        lambda *refs: main_kernel(names, *refs),
        out_shape=jax.ShapeDtypeStruct((6, 512, 128), F32),
        in_specs=[pl.BlockSpec(memory_space=pl.ANY)] * 2 + [pl.BlockSpec(memory_space=pltpu.VMEM)] * 2,
        out_specs=pl.BlockSpec(memory_space=pltpu.VMEM),
        scratch_shapes=list(scratch.values()),
        compiler_params=pltpu.CompilerParams(collective_id=0, has_side_effects=True, vmem_limit_bytes=56 * 2**20),
        name="section",
    )(conserved_fields.reshape(6, 512, 128), coeff, table, wave)
    return out.reshape(6, 16, 32, 128)


def solution(mesh):
    placed = (P(None, "gx", "gz", None), P(None, "gx", None, "gz", None), P())
    return jax.shard_map(
        local, mesh=mesh, in_specs=placed, out_specs=P(None, "gx", "gz", None), check_vma=False
    )
```

```python
import math

import jax, jax.numpy as jnp
from jax import lax
from jax.experimental import pallas as pl
from jax.experimental.pallas import tpu as pltpu
from jax.sharding import PartitionSpec as P
import numpy as np

F32 = jnp.float32
NXL, NZL, NYL = 16, 32, 128


def flux_parts(q, n):
    r, m1, m2, m3, en, ev = q
    rinv = 1.0 / r
    un = q[n] * rinv
    ke = (m1 * m1 + m2 * m2 + m3 * m3) * (0.5 * rinv)
    p = (en - ke - ev) * (1.0 / 2.5)
    s = jnp.abs(un) + jnp.sqrt(1.4 * (p * rinv))
    h = 0.5 * un
    g = [q[c] * h for c in range(6)]
    g[n] = g[n] + 0.5 * p
    g[4] = g[4] + p * h
    return g, 0.5 * s


def ratio(num, den):
    return num * pl.reciprocal(den, approx=False)


def correction(d2, d3, e0, e1, e2):
    d2s = d2 * d2 + 1e-6
    b0 = d2s + e0 * (d2 + (4.0 / 3.0) * e0)
    b1 = d2s + e1 * (d2 + (4.0 / 3.0) * e1)
    b2 = (d3 * d3 + 1e-6) + e2 * ((4.0 / 3.0) * e2 - d3)
    p0, p1, p2 = b0 * b0, b1 * b1, b2 * b2
    w0 = p1 * p2
    w1 = 6.0 * (p0 * p2)
    w2 = 3.0 * (p0 * p1)
    num = e0 * w0 + e1 * w1 + (e1 + 0.5 * (e1 - e2)) * w2
    return ratio(num, w0 + w1 + w2)


def face_value(a, gs, dg, dq, eg, eq):
    ad = [a * x for x in dq]
    ae = [a * x for x in eq]
    pd2, pd3 = dg[0] + ad[0], dg[1] + ad[1]
    md2, md3 = ad[2] - dg[2], ad[1] - dg[1]
    pe = [eg[i] + ae[i] for i in (0, 1, 2)]
    me = [eg[i] - ae[i] for i in (3, 2, 1)]
    lead = (gs - ad[1]) + 0.5 * (pd2 + md2)
    return lead + (1.0 / 3.0) * (correction(pd2, pd3, *pe) + correction(md2, md3, *me))


def face_sweep(qr, gr, ar, tr, comps, n, rows, unroll, tick):
    chunks = rows // 8

    def outer(t, _):
        c = t // chunks
        r0 = (t % chunks) * 8
        at = lambda ref, i: ref[c, pl.ds(pl.multiple_of(i * rows + r0, 8), 8), :]

        def advance(state, f):
            dq, dg, eq, eg = state
            dqn = at(qr, f + 5) - at(qr, f + 4)
            dgn = at(gr, f + 5) - at(gr, f + 4)
            eqn, egn = dqn - dq[2], dgn - dg[2]
            return (dq[0], dq[1], dq[2], dqn), (dg[0], dg[1], dg[2], dgn), (*eq, eqn), (*eg, egn)

        def one(state, f):
            dq, dg, eq, eg = advance(state, f)
            a = ar[pl.ds(pl.multiple_of(f * rows + r0, 8), 8), :]
            gs = at(gr, f + 2) + at(gr, f + 3)
            val = face_value(a, gs, dg[:3], dq[:3], eg, eq)
            return (dq[1:], dg[1:], eq[1:], eg[1:]), val

        qs = [at(qr, i) for i in range(5)]
        gs = [at(gr, i) for i in range(5)]
        dq = [qs[i + 1] - qs[i] for i in range(4)]
        dg = [gs[i + 1] - gs[i] for i in range(4)]
        eq = [dq[i + 1] - dq[i] for i in range(3)]
        eg = [dg[i + 1] - dg[i] for i in range(3)]
        state = (tuple(dq[1:]), tuple(dg[1:]), tuple(eq), tuple(eg))
        state, prev = one(state, 0)

        def inner(b, carry):
            state, prev = carry
            for k in range(unroll):
                f = b * unroll + k + 1
                state, val = one(state, f)
                tr[c, pl.ds(pl.multiple_of((f - 1) * rows + r0, 8), 8), :] = val - prev
                prev = val
            tick(t * (n // unroll) + b)
            return state, prev

        lax.fori_loop(0, n // unroll, inner, (state, prev))
        return 0

    lax.fori_loop(0, comps * chunks, outer, 0)


def speed_sweep(sr, ar, n, rows):
    def body(f, _):
        for r0 in range(0, rows, 8):
            ld = lambda i: sr[pl.ds(pl.multiple_of(i * rows + r0, 8), 8), :]
            m = ld(f)
            for o in range(1, 6):
                m = jnp.maximum(m, ld(f + o))
            ar[pl.ds(pl.multiple_of(f * rows + r0, 8), 8), :] = m
        return 0

    lax.fori_loop(0, n + 1, body, 0)


def flux_sweep(qr, gr, sr, first, count, normal):
    def body(i, _):
        at = pl.ds(pl.multiple_of(i * 8, 8), 8)
        g, s = flux_parts([qr[c, at, :] for c in range(6)], normal)
        for c in range(6):
            gr[c, at, :] = g[c]
        sr[at, :] = s
        return 0

    lax.fori_loop(first, first + count, body, 0, unroll=2)


def transpose_in(qx, tq, qy, gy, sy, tick):
    def block(blk, _):
        for c in range(6):
            x = qx[c, pl.ds(pl.multiple_of(96 + blk * 128, 32), 128), :]
            tq[c] = x.T

        def rows(y, _):
            y0 = pl.multiple_of(y * 8, 8)
            q = [tq[c, pl.ds(y0, 8), :] for c in range(6)]
            g, s = flux_parts(q, 2)
            base = (3 + y0) * 8
            for c in range(6):
                spot = pl.ds(base + (c % 2) * 4 + blk, 8, stride=8)
                qy[c // 2, spot, :] = q[c]
                gy[c // 2, spot, :] = g[c]
            sy[pl.ds(base + blk, 8, stride=8), :] = s
            sy[pl.ds(base + 4 + blk, 8, stride=8), :] = s
            return 0

        lax.fori_loop(0, 16, rows, 0)
        r, m1, m2, m3, en, ev = [tq[c, 0:8, :] for c in range(6)]
        rinv = 1.0 / r
        ke = (m1 * m1 + m2 * m2 + m3 * m3) * (0.5 * rinv)
        temp = (en - ke - ev) * (1.0 / 2.5) * rinv
        ghost = [r, -m1, -m2, -m3, en - 2.5 * r * (temp - 0.36 / temp), ev]
        g, s = flux_parts(ghost, 2)
        for k in range(3):
            for c in range(6):
                spot = pl.ds((2 - k) * 8 + (c % 2) * 4 + blk, 1)
                qy[c // 2, spot, :] = ghost[c][k : k + 1]
                gy[c // 2, spot, :] = g[c][k : k + 1]
            sy[pl.ds((2 - k) * 8 + blk, 1), :] = s[k : k + 1]
            sy[pl.ds((2 - k) * 8 + 4 + blk, 1), :] = s[k : k + 1]
        tick(blk)
        return 0

    lax.fori_loop(0, 4, block, 0)
    for k in range(3):
        src, dst = pl.ds(130 * 8, 8), pl.ds((131 + k) * 8, 8)
        for c in range(3):
            qy[c, dst, :] = qy[c, src, :]
            gy[c, dst, :] = gy[c, src, :]
        sy[dst, :] = sy[src, :]


def swap_in(qx, qz):
    def body(z, _):
        for c in range(6):
            for x0 in (0, 8):
                v = qx[c, pl.ds((3 + x0) * 32 + z, 8, stride=32), :]
                qz[c, pl.ds(pl.multiple_of((3 + z) * 16 + x0, 8), 8), :] = v
        return 0

    lax.fori_loop(0, 32, body, 0)


def combine(qx, tx, tz, ty, src, out, strength):
    def block(blk, _):
        for c in range(6):
            t = ty[c // 2, pl.ds((c % 2) * 4 + blk, 128, stride=8), :].T
            for k in range(4):
                x = blk * 4 + k
                span = tz[c, pl.ds(x, 32, stride=16), :]
                at = pl.ds(pl.multiple_of(x * 32, 32), 32)
                q = qx[c, pl.ds(pl.multiple_of(96 + x * 32, 32), 32), :]
                rate = tx[c, at, :] + span + t[k * 32 : k * 32 + 32] + strength(x) * q
                if c == 5:
                    rate = rate - src[blk, k * 32 : k * 32 + 32, :]
                out[c, at, :] = q - 0.05 * rate
        return 0

    lax.fori_loop(0, 4, block, 0)


def relaxation(qx, src):
    def relax(i, _):
        at = pl.ds(pl.multiple_of(96 + i * 8, 8), 8)
        r, m1, m2, m3, en, ev = [qx[c, at, :] for c in range(6)]
        rinv = 1.0 / r
        ke = (m1 * m1 + m2 * m2 + m3 * m3) * (0.5 * rinv)
        p = (en - ke - ev) * (1.0 / 2.5)
        temp = p * rinv
        eq = 2.0 / (jnp.exp(2.0 / temp) - 1.0)
        tau = 0.5 * jnp.exp(1.5 * (jnp.exp(jnp.log(temp) * (-1.0 / 3.0)) - 1.0))
        src[i // 16, pl.ds(pl.multiple_of(i % 16 * 8, 8), 8), :] = (r * eq - ev) * p / tau
        return 0

    lax.fori_loop(0, 64, relax, 0, unroll=2)


def weno_scratch():
    v = lambda *s: pltpu.VMEM(s, F32)
    return dict(
        qx=v(6, 22 * 32, 128), gx=v(6, 22 * 32, 128), sx=v(22 * 32, 128), ax=v(17 * 32, 128), tx=v(6, 16 * 32, 128),
        qz=v(6, 38 * 16, 128), gz=v(6, 38 * 16, 128), sz=v(38 * 16, 128), az=v(33 * 16, 128), tz=v(6, 32 * 16, 128),
        tq=v(6, 128, 128), qy=v(3, 134 * 8, 128), gy=v(3, 134 * 8, 128), sy=v(134 * 8, 128), ay=v(129 * 8, 128), ty=v(3, 128 * 8, 128),
    )


MESH = pl.DeviceIdType.MESH
PLANES = 25
STEP = 2
HOP = 11
PIECES = 24
WIRE_TICKS = PIECES * STEP + 8 * HOP


def kron_table(wave, kron):
    iota = lambda shape, d: lax.broadcasted_iota(jnp.int32, shape, d)
    rows = jnp.where(iota((224, 32), 0) // 8 == iota((224, 32), 1), 1.0, 0.0).astype(jnp.bfloat16)
    col = iota((128, 1024), 1)
    cols = jnp.where(col // 512 * 64 + col % 512 // 8 == iota((128, 1024), 0), 1.0, 0.0).astype(jnp.bfloat16)
    wide = jnp.dot(wave[...], cols, preferred_element_type=F32).astype(jnp.bfloat16)
    wide = jnp.dot(rows, wide, preferred_element_type=F32)
    kron[...] = jnp.where(iota((224, 1024), 0) % 8 == iota((224, 1024), 1) % 8, wide, 0.0).astype(jnp.bfloat16)


def spectral(i, raw, rows, table, kron, modes, sums, put, tick):
    for p in range(2):
        rows[:, p * 512 : p * 512 + 512] = raw[i % 2, p].reshape(512, 512)
    for h in range(2):
        for p in range(2):
            at = p * 512 + h * 256
            span = jnp.dot(rows[...], table[:, at : at + 256], preferred_element_type=F32)
            modes[p * 512 : p * 512 + 512, :] = span.astype(jnp.bfloat16)
            tick(h * 3 + p)
        sums[:, h * 256 : h * 256 + 256] = jnp.dot(kron[...], modes[...], preferred_element_type=F32)
        tick(h * 3 + 2)
    lane = lax.broadcasted_iota(jnp.int32, (8, 128), 1)
    low64 = lane < 64
    low32 = lane % 64 < 32
    for g in range(7):
        for jb in range(4):
            f = [sums[g * 32 + n * 8 : g * 32 + n * 8 + 8, jb * 128 : jb * 128 + 128] for n in range(4)]
            n0 = jnp.where(low64, f[0], pltpu.roll(f[2], 64, 1))
            n2 = jnp.where(low64, pltpu.roll(f[0], 64, 1), f[2])
            n1 = jnp.where(low64, f[1], pltpu.roll(f[3], 64, 1))
            n3 = jnp.where(low64, pltpu.roll(f[1], 64, 1), f[3])
            for k, (a, b) in enumerate(((n0, n1), (n2, n3))):
                put(4 * jb + 2 * k, g, jnp.where(low32, a, pltpu.roll(b, 32, 1)))
                put(4 * jb + 2 * k + 1, g, jnp.where(low32, pltpu.roll(a, 96, 1), b))


def tables(feed_plane):
    n = np.arange(512)
    angle = 2.0 * np.pi / 512.0 * ((n[:, None] * n[None, :]) % 512)
    cz, sz = np.cos(angle), np.sin(angle)
    table = jnp.asarray(np.block([[cz, sz], [-sz, cz]]).astype(np.float32)).astype(jnp.bfloat16)
    plane, col = (lax.broadcasted_iota(jnp.int32, (32, 128), d) for d in range(2))
    feed = jnp.pad(feed_plane, (0, 32 - PLANES)).reshape(32, 1)
    mode = lax.axis_index("gx") * 64 + col % 64
    ids = (feed * mode + 512 * (col // 64)) % 2048
    wave = jnp.cos(2.0 * math.pi / 2048 * ids.astype(F32))
    return table, jnp.where(plane < PLANES, wave, 0.0).astype(jnp.bfloat16)


def main_kernel(names, q_hbm, coeff, table, wave, out, *scratch):
    s = dict(zip(names, scratch))
    part = s["part"]
    qx, qz, land, swap, feed = s["qx"], s["qz"], s["land"], s["swap"], s["feed"]
    gx, gz = lax.axis_index("gx"), lax.axis_index("gz")
    z, xlo = gx % 8, gx // 8
    z_next = {0: xlo * 8 + (z + 1) % 8, 1: xlo * 8 + (z + 7) % 8}
    is_root = z < 2

    load = pltpu.make_async_copy(q_hbm, qx.at[:, 96:608], s["load_sem"])
    load.start()

    def fetch(i):
        v = jnp.where(i < 3, 3 - 3 * xlo, 3 * xlo) + i % 3
        return pltpu.make_async_copy(coeff.at[:, :, v], s["raw"].at[i % 2], s["raw_sem"].at[i % 2])

    fetch(0).start()
    fetch(1).start()
    kron_table(wave, s["kron"])

    barrier = pltpu.get_barrier_semaphore()

    def greet(a, b):
        pl.semaphore_signal(barrier, inc=1, device_id=(a, b), device_id_type=MESH)

    @pl.when(gx < 15)
    def _():
        greet(gx + 1, gz)

    @pl.when(gx > 0)
    def _():
        greet(gx - 1, gz)

    greet((gx + 8) % 16, gz)
    greet(z_next[0], gz)
    greet(z_next[1], gz)
    greet(gx, (gz + 1) % 16)
    greet(gx, (gz + 15) % 16)

    @pl.when(is_root)
    def _():
        def each(b, _):
            @pl.when((xlo == 1) | (b != gz))
            def _():
                greet(z, b)

            @pl.when(xlo == 0)
            def _():
                greet(8 + z, b)

            return 0

        lax.fori_loop(0, 16, each, 0)

    ends = jnp.where((gx == 0) | (gx == 15), 1, 0)
    roots = jnp.where(is_root, jnp.where(xlo == 0, 31, 16), 0)
    pl.semaphore_wait(barrier, 7 - ends + roots)

    def remote(src, dst, ssem, rsem, a, b):
        return pltpu.make_async_remote_copy(
            src_ref=src, dst_ref=dst, send_sem=ssem, recv_sem=rsem, device_id=(a, b), device_id_type=MESH
        )

    groups = (slice(0, 4), slice(4, 7))
    every = slice(0, 7)
    lines = ((0, (z + 7) % 8), (1, (8 - z) % 8))

    def exchange(d, i):
        block = (i // 2, pl.ds(8 * d + i % 2 * 4, 4))
        return remote(part.at[1 - xlo, *block], swap.at[block], s["swap_send"], s["swap_recv"].at[d, i], (gx + 8) % 16, gz)

    def tick(n):
        for d, pos in lines:
            first, second = groups[d], groups[1 - d]

            def turn(k, last):
                v, e = k // 8, 8 * d + k % 8
                held = lambda g: land.at[v, e, g]
                mine = lambda g: part[xlo, v, e, g] + swap[v, e, g]
                ssem, rsem = s["send_sem"].at[d], s["recv_sem"].at[d, k]
                onward = lambda g: remote(held(g), held(g), ssem, rsem, z_next[d], gz)

                def add(g):
                    held(g)[...] = held(g)[...] + mine(g)

                def deliver(r):
                    c = (gz + e) % 16
                    place = feed.at[3 * xlo + v, gz, 0 : 4 - r]
                    here = (xlo == 0) & (c == gz)

                    @pl.when(here)
                    def _():
                        pltpu.make_async_copy(held(groups[r]), place, s["feed_sem"]).start()

                    @pl.when(jnp.logical_not(here))
                    def _():
                        remote(held(groups[r]), place, ssem, s["feed_sem"], r, c).start()

                if last:
                    onward(second).wait_recv()
                    add(second)
                    deliver(1 - d)
                    return

                @pl.when(k % 4 == 0)
                def _():
                    exchange(d, k // 4).wait_recv()

                @pl.when(pos == 0)
                def _():
                    held(first)[...] = mine(first)
                    onward(first).start()

                @pl.when(pos == 1)
                def _():
                    held(second)[...] = mine(second)
                    onward(first).wait_recv()
                    add(first)
                    onward(every).start()

                @pl.when((pos > 1) & (pos < 7))
                def _():
                    onward(every).wait_recv()
                    add(every)
                    onward(every).start()

                @pl.when(pos == 7)
                def _():
                    onward(every).wait_recv()
                    add(every)
                    onward(second).start()
                    deliver(d)

            def due(place, ok, last):
                m = n - place * HOP
                pl.when(ok & (m >= 0) & (m < PIECES * STEP) & (m % STEP == 0))(lambda: turn(m // STEP, last))

            due(pos, pos >= 0, False)
            due(8, pos == 0, True)

    halo = []
    for i, (src, dst, a, b, ok_send, ok_recv) in enumerate(
        (
            (qx.at[:, 512:608], qx.at[:, 0:96], jnp.minimum(gx + 1, 15), gz, gx < 15, gx > 0),
            (qx.at[:, 96:192], qx.at[:, 608:704], jnp.maximum(gx - 1, 0), gz, gx > 0, gx < 15),
            (qz.at[:, 512:560], qz.at[:, 0:48], gx, (gz + 1) % 16, None, None),
            (qz.at[:, 48:96], qz.at[:, 560:608], gx, (gz + 15) % 16, None, None),
        )
    ):
        halo.append((remote(src, dst, s["halo_send"].at[i], s["halo_recv"].at[i], a, b), ok_send, ok_recv))

    def on(ok, act):
        if ok is None:
            act()
        else:
            pl.when(ok)(act)

    load.wait()
    for copy, ok, _ in halo[:2]:
        on(ok, copy.start)
    swap_in(qx, qz)
    for copy, ok, _ in halo[2:]:
        on(ok, copy.start)

    def variable(i, _):
        half = jnp.where(i < 3, 1 - xlo, xlo)
        fetch(i).wait()

        def put(c, g, tile):
            part[half, i % 3, (c + 16 - gz) % 16, g] = tile

        spectral(i, s["raw"], s["rows"], table, s["kron"], s["modes"], s["sums"], put, lambda j: tick((i - 4) * 6 + j))

        @pl.when(i < 4)
        def _():
            fetch(i + 2).start()

        @pl.when(i < 3)
        def _():
            for h in range(2):
                for d in range(2):
                    exchange(d, i * 2 + h).start()

        return 0

    lax.fori_loop(0, 6, variable, 0)
    transpose_in(qx, s["tq"], s["qy"], s["gy"], s["sy"], lambda blk: tick(blk + 12))
    relaxation(qx, s["tq"])
    speed_sweep(s["sy"], s["ay"], 128, 8)
    face_sweep(s["qy"], s["gy"], s["ay"], s["ty"], 3, 128, 8, 8, lambda i: tick(i + 16))
    for copy, _, ok in halo[2:]:
        on(ok, copy.wait_recv)
    flux_sweep(qz, s["gz"], s["sz"], 0, 76, 3)
    speed_sweep(s["sz"], s["az"], 32, 16)
    face_sweep(qz, s["gz"], s["az"], s["tz"], 6, 32, 16, 8, lambda i: tick(i + 64))
    for copy, _, ok in halo[:2]:
        on(ok, copy.wait_recv)

    @pl.when(gx == 0)
    def _():
        for i in range(3):
            qx[:, i * 32 : i * 32 + 32] = qx[:, 96:128]

    @pl.when(gx == 15)
    def _():
        for i in range(3):
            qx[:, 608 + i * 32 : 640 + i * 32] = qx[:, 576:608]

    flux_sweep(qx, s["gx"], s["sx"], 0, 88, 1)
    speed_sweep(s["sx"], s["ax"], 16, 32)
    face_sweep(qx, s["gx"], s["ax"], s["tx"], 6, 16, 32, 16, lambda i: tick(i + 112))

    def strength(x):
        plane = gx * 16 + x
        level = 1.0 - plane.astype(F32) * (1.0 / PLANES)
        return jnp.where(plane < PLANES, 2.0 * level * level, 0.0)

    combine(qx, s["tx"], s["tz"], s["ty"], s["tq"], out, strength)

    def drain(n, _):
        tick(n)
        return 0

    lax.fori_loop(136, WIRE_TICKS, drain, 0)

    for r in range(2):

        @pl.when(gx == r)
        def _():
            count = 4 if r == 0 else 3
            whole = feed.at[:, :, 0:count]
            pltpu.make_async_copy(whole, whole, s["feed_sem"]).wait()

            def add(v, _):
                for g in range(count):
                    t = feed[v, :, g].reshape(128, 128).T
                    for i in range(4):
                        x = g * 4 + i
                        at = slice(x * 32, x * 32 + 32)
                        out[v, at, :] = out[v, at, :] + (0.05 * strength(jnp.int32(x))) * t[i * 32 : i * 32 + 32]
                return 0

            lax.fori_loop(0, 6, add, 0)

    for copy, ok, _ in halo:
        on(ok, copy.wait_send)
    pltpu.make_async_copy(swap, swap, s["swap_send"]).wait()
    for d, pos in lines:

        def sent(blocks, g):
            span = land.at[:, blocks, g]
            pltpu.make_async_copy(span, span, s["send_sem"].at[d]).wait()

        if d == 1:
            sent(slice(0, 8), every)
        else:
            sent(slice(0, 7), every)
            own = xlo == 0
            pl.when(own & (pos == 0))(lambda: sent(slice(7, 8), groups[0]))
            pl.when(own & (pos == 7))(lambda: sent(slice(7, 8), groups[1]))
            pl.when(jnp.logical_not(own) | ((pos > 0) & (pos < 7)))(lambda: sent(slice(7, 8), every))


def local(conserved_fields, coeff, feed_plane):
    table, wave = tables(feed_plane)
    scratch = weno_scratch()
    scratch.update(
        raw=pltpu.VMEM((2, 2, 64, 8, 512), jnp.bfloat16),
        rows=pltpu.VMEM((512, 1024), jnp.bfloat16),
        kron=pltpu.VMEM((224, 1024), jnp.bfloat16),
        modes=pltpu.VMEM((1024, 256), jnp.bfloat16),
        sums=pltpu.VMEM((224, 512), F32),
        part=pltpu.VMEM((2, 3, 16, 7, 8, 128), F32),
        raw_sem=pltpu.SemaphoreType.DMA((2,)),
        land=pltpu.VMEM((3, 16, 7, 8, 128), F32),
        swap=pltpu.VMEM((3, 16, 7, 8, 128), F32),
        feed=pltpu.VMEM((6, 16, 4, 8, 128), F32),
        load_sem=pltpu.SemaphoreType.DMA,
        halo_send=pltpu.SemaphoreType.DMA((4,)),
        halo_recv=pltpu.SemaphoreType.DMA((4,)),
        send_sem=pltpu.SemaphoreType.DMA((2,)),
        recv_sem=pltpu.SemaphoreType.DMA((2, PIECES)),
        swap_send=pltpu.SemaphoreType.DMA,
        swap_recv=pltpu.SemaphoreType.DMA((2, 6)),
        feed_sem=pltpu.SemaphoreType.DMA,
    )
    names = list(scratch)
    out = pl.pallas_call(
        lambda *refs: main_kernel(names, *refs),
        out_shape=jax.ShapeDtypeStruct((6, 512, 128), F32),
        in_specs=[pl.BlockSpec(memory_space=pl.ANY)] * 2 + [pl.BlockSpec(memory_space=pltpu.VMEM)] * 2,
        out_specs=pl.BlockSpec(memory_space=pltpu.VMEM),
        scratch_shapes=list(scratch.values()),
        compiler_params=pltpu.CompilerParams(collective_id=0, has_side_effects=True, vmem_limit_bytes=56 * 2**20),
        name="section",
    )(conserved_fields.reshape(6, 512, 128), coeff, table, wave)
    return out.reshape(6, 16, 32, 128)


def solution(mesh):
    placed = (P(None, "gx", "gz", None), P(None, "gx", None, "gz", None), P())
    return jax.shard_map(
        local, mesh=mesh, in_specs=placed, out_specs=P(None, "gx", "gz", None), check_vma=False
    )
```
